32 devices in a mesh: seq: 32 (over z, y, x, core).
Axes of the slice: x: 2, y: 2, z: 4, core: 2. Of those that a mesh axis runs over, the one named last changes fastest.
Arguments:
- rhs: float32 [4096, 2048], P('seq'), may hold values from -17 to 17
- rate: float32 [16, 2048], replicated, may hold values from 9.765625e-05 to 0.0333333333, as said below
- delta: float32 [4096, 2048], P('seq'), may hold values from 0.25 to 2048, as said below
- b_proj: float32 [4096, 16], P('seq'), may hold values from -1 to 3
- c_proj: float32 [4096, 16], P('seq'), may hold values from -0.21 to 0.33
- skip: float32 [2048], replicated, may hold values from 0.5 to 1.5
- curvature: float32 [4096, 2048], P('seq'), may hold values from 0.3 to 3
- damping: float32 [2048], replicated, may hold values from 0.1 to 1
Outputs:
- solution: float32 [4096, 2048], P('seq')
- residual: float32 [4096, 2048], P('seq')
The draws below stay inside these ranges and needn't reach their ends.
Inputs may be any that keep to these rules, and one draw needn't show every extreme that they name: `rate`: all entries positive. `delta`: all entries positive.
All inputs are finite; a program needn't handle non-finite values.
Results may differ from the reference program's by a relative error of at most 0.0003.
Values sent between devices are 32-bit elements; how exact they have to be, the bound alone decides.
No kernel may reach another device: no remote copies, remote signals or barrier semaphores. Data moves between devices by JAX's collectives and lax.ppermute only.
A program may use at most 192 MiB of HBM per device.

```python
import math
import jax
import jax.numpy as jnp
from jax import lax

INNER_CHANNELS = 2048
STATE = 16
TOK_DEV = 128
CG_ITERS = 2
SEQUENCE_TOKENS = 4096


def draw_rate(key, part):
    key_mask, key_slow, key_fast = jax.random.split(jax.random.fold_in(key, 11), 3)
    share = 0.5
    slow_mask = jax.random.uniform(key_mask, (INNER_CHANNELS,), jnp.float32) < share
    slow_rate = jax.random.uniform(key_slow, (STATE, INNER_CHANNELS), jnp.float32, 0.4, 1.2) / SEQUENCE_TOKENS
    fast_rate = jax.random.uniform(key_fast, (STATE, INNER_CHANNELS), jnp.float32, 1.0 / 60.0, 1.0 / 30.0)
    return jnp.where(slow_mask[None, :], slow_rate, fast_rate).astype(jnp.float32)


def draw_delta(key, part):
    key_rough, key_block, key_where, key_length = jax.random.split(jax.random.fold_in(key, 23), 4)
    rough = jax.random.uniform(key_rough, (SEQUENCE_TOKENS, INNER_CHANNELS), jnp.float32, 0.5, 1.5)
    blocks = SEQUENCE_TOKENS // TOK_DEV
    block_scale = jnp.exp(jax.random.uniform(key_block, (blocks, 1, 1), jnp.float32, -0.693, 0.693))
    drawn_spacing = (rough.reshape(blocks, TOK_DEV, INNER_CHANNELS) * block_scale).reshape(SEQUENCE_TOKENS, INNER_CHANNELS)
    drawn_spacing = jnp.maximum(drawn_spacing, 0.25)
    token_slots = jax.random.randint(key_where, (2,), 0, SEQUENCE_TOKENS)
    token_positions = jnp.arange(SEQUENCE_TOKENS)
    token_group = jnp.any(token_positions[:, None] == token_slots[None, :], axis=1)
    token_group_size = SEQUENCE_TOKENS * jax.random.uniform(key_length, (SEQUENCE_TOKENS, INNER_CHANNELS), jnp.float32, 0.3, 0.5)
    return jnp.where(token_group[:, None], token_group_size, drawn_spacing).astype(jnp.float32)


def draw_rhs(key, part):
    key_main = jax.random.fold_in(jax.random.fold_in(key, 37), 0)
    token_positions = jnp.arange(SEQUENCE_TOKENS).astype(jnp.float32) / SEQUENCE_TOKENS
    ramp = 1.0 + 2.0 * token_positions
    values = jax.random.truncated_normal(key_main, -5.0, 5.0, (SEQUENCE_TOKENS, INNER_CHANNELS), jnp.float32) + 0.5
    return (values * ramp[:, None]).astype(jnp.float32)


def draw_b_proj(key, part):
    key_base, key_rough = jax.random.split(jax.random.fold_in(key, 41))
    base = jax.random.uniform(key_base, (STATE,), jnp.float32, 0.5, 1.5)
    rough = 0.5 * jax.random.truncated_normal(key_rough, -3.0, 3.0, (SEQUENCE_TOKENS, STATE), jnp.float32)
    return (base[None, :] + rough).astype(jnp.float32)


def draw_c_proj(key, part):
    key_base, key_rough = jax.random.split(jax.random.fold_in(key, 53))
    base = jax.random.uniform(key_base, (STATE,), jnp.float32, 0.03, 0.09)
    rough = 0.08 * jax.random.truncated_normal(key_rough, -3.0, 3.0, (SEQUENCE_TOKENS, STATE), jnp.float32)
    return (base[None, :] + rough).astype(jnp.float32)


def steps_of(stream_key, shape, cuts, least, largest):
    loudness, own = 1.0, jax.random.fold_in(stream_key, 6)
    for position, shards_of in cuts:
        heights = jnp.exp(jax.random.uniform(jax.random.fold_in(own, position), (shards_of,), jnp.float32, least / len(cuts), largest / len(cuts)))
        loudness = loudness * jnp.repeat(heights, shape[position] // shards_of).reshape([-1 if axis == position else 1 for axis in range(len(shape))])
    return loudness


def setup_inputs(seed: int = 0) -> dict:
    key_list = jax.random.split(jax.random.key(seed), 9)
    return {
        "rhs": draw_rhs(jax.random.fold_in(key_list[8], 71), 0),
        "rate": draw_rate(jax.random.fold_in(key_list[8], 71), 0),
        "delta": draw_delta(jax.random.fold_in(key_list[8], 71), 0),
        "b_proj": draw_b_proj(jax.random.fold_in(key_list[8], 71), 0),
        "c_proj": draw_c_proj(jax.random.fold_in(key_list[8], 71), 0),
        "skip": jnp.clip(1.0 + 0.1 * jax.random.normal(key_list[5], (INNER_CHANNELS,), jnp.float32), 0.5, 1.5),
        "curvature": jnp.clip(jnp.exp(math.log(3.0) - 2.3025851 * jax.random.uniform(key_list[6], (SEQUENCE_TOKENS, INNER_CHANNELS), jnp.float32) ** steps_of(key_list[6], (SEQUENCE_TOKENS, INNER_CHANNELS), ((0, 32),), -0.2, 0.2)), 0.3, 3.0),
        "damping": jnp.clip(jnp.exp(jax.random.uniform(key_list[7], (INNER_CHANNELS,), jnp.float32, math.log(0.1), math.log(1.0))), 0.1, 1.0),
    }


def tangent_map(vector, rate, delta, b_proj, c_proj, skip):
    def advance(state, inputs):
        delta_row, b_row, c_row, v_row = inputs
        exponent = delta_row[None, :] * rate
        state = jnp.exp(-exponent) * state - jnp.expm1(-exponent) * (b_row[:, None] * v_row[None, :])
        return state, jnp.sum(c_row[:, None] * state, axis=0)

    start_state = jnp.zeros(rate.shape, jnp.float32)
    _, output = lax.scan(advance, start_state, (delta, b_proj, c_proj, vector))
    return output + skip[None, :] * vector


def adjoint_map(weights, rate, delta, b_proj, c_proj, skip):
    def retreat(passed, inputs):
        delta_row, b_row, c_row, w_row = inputs
        exponent = delta_row[None, :] * rate
        costate = c_row[:, None] * w_row[None, :] + passed
        gained = -jnp.expm1(-exponent) * costate
        return jnp.exp(-exponent) * costate, jnp.sum(b_row[:, None] * gained, axis=0)

    start_state = jnp.zeros(rate.shape, jnp.float32)
    _, output = lax.scan(retreat, start_state, (delta, b_proj, c_proj, weights), reverse=True)
    return output + skip[None, :] * weights


def reference(rhs, rate, delta, b_proj, c_proj, skip, curvature, damping):
    def damped_product(vector):
        forward = tangent_map(vector, rate, delta, b_proj, c_proj, skip)
        return adjoint_map(curvature * forward, rate, delta, b_proj, c_proj, skip) + damping[None, :] * vector

    solution = jnp.zeros_like(rhs)
    residual = rhs
    direction = rhs
    norm_now = jnp.sum(residual * residual)
    for iteration in range(CG_ITERS):
        curved = damped_product(direction)
        step_size = norm_now / jnp.sum(direction * curved)
        solution = solution + step_size * direction
        residual = residual - step_size * curved
        norm_next = jnp.sum(residual * residual)
        direction = residual + (norm_next / norm_now) * direction
        norm_now = norm_next
    return solution, residual
```

```python
import functools

import jax
import jax.numpy as jnp
from jax import lax
from jax.experimental import pallas as pl
from jax.experimental.pallas import tpu as pltpu
from jax.sharding import PartitionSpec as P

SUB, LANE = 8, 128
LOG2E = 1.4426950408889634
LN2 = 0.6931471805599453
SMALL = 0.03
G1, G2, G3 = LN2, LN2 * LN2 / 2.0, LN2 * LN2 * LN2 / 6.0
F32 = jnp.float32


def gain_of(z):
    near = -z * (G1 + z * (G2 + z * G3))
    return jnp.where(z > -SMALL, near, 1.0 - jnp.exp2(z))


def sub_index():
    return lax.broadcasted_iota(jnp.int32, (SUB, LANE), 0)


def spread(row):
    return jnp.broadcast_to(row, (SUB, LANE))


def rolled(x, shift):
    return pltpu.roll(x, shift % SUB, 0)


def scan_chunks(value, decay, backward):
    at = sub_index()
    edge = at == (SUB - 1 if backward else 0)
    keep = jnp.where(edge, 0.0, decay)
    for step in (1, 2, 4):
        shift = -step if backward else step
        value = value + keep * rolled(value, shift)
        if step < 4:
            keep = keep * rolled(keep, shift)
    entering = jnp.where(edge, 0.0, rolled(value, -1 if backward else 1))
    last = value[0:1] if backward else value[SUB - 1 : SUB]
    return entering, last


def totals_around(total):
    at = sub_index()
    before = jnp.zeros_like(total)
    after = jnp.zeros_like(total)
    for step in range(1, SUB):
        before = before + jnp.where(at >= step, rolled(total, step), 0.0)
        after = after + jnp.where(at < SUB - step, rolled(total, -step), 0.0)
    return before, after


def summed(parts):
    while len(parts) > 1:
        parts = [sum(parts[i : i + 2]) for i in range(0, len(parts), 2)]
    return parts[0]


class Sizes:
    def __init__(self, tokens, columns, entries, devices):
        self.tokens, self.columns = tokens, columns
        self.entries, self.devices = entries, devices
        self.steps = tokens // SUB
        self.blocks = columns // LANE
        self.rows = entries * self.blocks // devices


def cols(block):
    return pl.ds(pl.multiple_of(block * LANE, LANE), LANE)


def write_state(s, ref, block, rows_of):
    per = s.entries // s.rows
    for piece in range(per):
        where = block * per + piece
        for row in range(s.rows):
            ref[where, row : row + 1, :] = rows_of[piece * s.rows + row]


def read_state(s, ref, block):
    per = s.entries // s.rows
    out = []
    for piece in range(per):
        where = block * per + piece
        for row in range(s.rows):
            out.append(spread(ref[where, row : row + 1, :]))
    return out


def load_rates(s, rate_ref, block):
    return [
        spread(rate_ref[n : n + 1, cols(block)]) * (-LOG2E) for n in range(s.entries)
    ]


def forward_summary(s, block, get_v, gain_ref, bx_ref, rates, total, e_ref, put):
    state = [jnp.zeros((SUB, LANE), F32)] * s.entries
    for j in range(s.steps):
        v = get_v(j)
        for n in range(s.entries):
            state[n] = state[n] + gain_ref[block, j, n] * (bx_ref[j, n] * v - state[n])
    finish_summary(s, block, state, rates, total, e_ref, put, False)


def backward_summary(s, block, get_w, gain_ref, cx_ref, rates, total, e_ref, put):
    passed = [jnp.zeros((SUB, LANE), F32)] * s.entries
    for j in reversed(range(s.steps)):
        w = get_w(j)
        for n in range(s.entries):
            costate = cx_ref[j, n] * w + passed[n]
            passed[n] = costate - gain_ref[block, j, n] * costate
    finish_summary(s, block, passed, rates, total, e_ref, put, True)


def finish_summary(s, block, state, rates, total, e_ref, put, backward):
    lasts = []
    for n in range(s.entries):
        entering, last = scan_chunks(
            state[n], jnp.exp2(total * rates[n]), backward
        )
        e_ref[block, n] = entering
        lasts.append(last)
    write_state(s, put, block, lasts)


def first_kernel(
    s, rhs_ref, delta_ref, rate_ref, b_ref, c_ref,
    gain_ref, bx_ref, cx_ref, total_ref, e_ref, out_ref, tile_v, tile_d,
):
    for j in range(s.steps):
        rows = pl.ds(j, SUB, stride=s.steps)
        b, c = b_ref[rows, :], c_ref[rows, :]
        for n in range(s.entries):
            bx_ref[j, n] = jnp.broadcast_to(b[:, n : n + 1], (SUB, LANE))
            cx_ref[j, n] = jnp.broadcast_to(c[:, n : n + 1], (SUB, LANE))

    def body(block, carry):
        tile_v[...] = rhs_ref[:, cols(block)]
        tile_d[...] = delta_ref[:, cols(block)]
        rates = load_rates(s, rate_ref, block)
        total = jnp.zeros((SUB, LANE), F32)
        for j in range(s.steps):
            d = tile_d[pl.ds(j, SUB, stride=s.steps), :]
            total = total + d
            for n in range(s.entries):
                gain_ref[block, j, n] = gain_of(d * rates[n])
        total_ref[block] = total

        def get_v(j):
            return tile_v[pl.ds(j, SUB, stride=s.steps), :]

        forward_summary(
            s, block, get_v, gain_ref, bx_ref, rates, total, e_ref, out_ref
        )
        whole = jnp.sum(total, axis=0, keepdims=True)
        per = s.entries // s.rows
        for n in range(s.entries):
            out_ref[
                block * per + n // s.rows,
                s.rows + n % s.rows : s.rows + n % s.rows + 1,
                :,
            ] = jnp.exp2(whole * rates[n][0:1])
        return carry

    lax.fori_loop(0, s.blocks, body, 0)


def put_sums(s, out_ref, first, second):
    first = jnp.sum(first, axis=0, keepdims=True)
    second = jnp.sum(second, axis=0, keepdims=True)

    def body(device, carry):
        out_ref[device, s.rows : s.rows + 1, :] = first
        out_ref[device, s.rows + 1 : s.rows + 2, :] = second
        return carry

    lax.fori_loop(0, s.devices, body, 0)


def link_kernel(s, backward, has_sums, got_ref, decay_ref, arrive_ref, sums_ref):
    carried = jnp.zeros((s.rows, LANE), F32)
    first = jnp.zeros((1, LANE), F32)
    second = jnp.zeros((1, LANE), F32)
    order = range(s.devices)
    for device in reversed(order) if backward else order:
        arrive_ref[device] = carried
        carried = (
            decay_ref[device, s.rows : 2 * s.rows, :] * carried
            + got_ref[device, 0 : s.rows, :]
        )
        if has_sums:
            first = first + got_ref[device, s.rows : s.rows + 1, :]
            second = second + got_ref[device, s.rows + 1 : s.rows + 2, :]
    sums_ref[0] = spread(jnp.sum(first, axis=1, keepdims=True))
    sums_ref[1] = spread(jnp.sum(second, axis=1, keepdims=True))


def enter(s, arrive_ref, e_ref, block, rates, around):
    arrive = read_state(s, arrive_ref, block)
    return [
        e_ref[block, n] + jnp.exp2(around * rates[n]) * arrive[n]
        for n in range(s.entries)
    ]


def forward_kernel(s, first, *refs):
    refs = list(refs)
    v_ref, curv_ref, rate_ref, skip_ref, damp_ref = refs[:5]
    gain_ref, bx_ref, cx_ref, total_ref, e_in, arrive_ref = refs[5:11]
    refs = refs[11:]
    if not first:
        rhs_ref, y0_ref, sums_b, sums_c = refs[:4]
        refs = refs[4:]
        ratio = sums_c[0] / sums_b[0]
    e_out, out_ref, w_ref = refs[:3]
    refs = refs[3:]
    y_ref, tile_v, tile_c = refs if first else (refs[0], refs[1], refs[2])

    def body(block, carry):
        squares, inner = carry
        tile_c[...] = curv_ref[:, cols(block)]
        if first:
            tile_v[...] = v_ref[:, cols(block)]
        else:
            tile_v[...] = rhs_ref[:, cols(block)]
        rates = load_rates(s, rate_ref, block)
        total = total_ref[block]
        before, after = totals_around(total)
        skip = spread(skip_ref[0:1, cols(block)])
        damp = spread(damp_ref[0:1, cols(block)])
        state = enter(s, arrive_ref, e_in, block, rates, before)
        for j in range(s.steps):
            rows = pl.ds(j, SUB, stride=s.steps)
            v = tile_v[rows, :] if first else v_ref[block, j]
            parts = [skip * v]
            for n in range(s.entries):
                state[n] = state[n] + gain_ref[block, j, n] * (
                    bx_ref[j, n] * v - state[n]
                )
                parts.append(cx_ref[j, n] * state[n])
            y = summed(parts)
            if first:
                y_ref[block, j] = y
                squares = squares + v * v
                along = v
            else:
                y = y + ratio * y0_ref[block, j]
                along = v + ratio * tile_v[rows, :]
                y_ref[block, j] = along
            w = tile_c[rows, :] * y
            w_ref[block, j] = w
            inner = inner + (w * y + damp * (along * along))

        def get_w(j):
            return w_ref[block, j]

        backward_summary(
            s, block, get_w, gain_ref, cx_ref, rates, total, e_out, out_ref
        )
        return squares, inner

    zero = jnp.zeros((SUB, LANE), F32)
    squares, inner = lax.fori_loop(0, s.blocks, body, (zero, zero))
    put_sums(s, out_ref, squares, inner)


def backward_block(s, block, w_ref, skip, gain_ref, bx_ref, cx_ref, passed, use):
    for j in reversed(range(s.steps)):
        w = w_ref[block, j]
        parts = [skip * w]
        for n in range(s.entries):
            costate = cx_ref[j, n] * w + passed[n]
            gained = gain_ref[block, j, n] * costate
            passed[n] = costate - gained
            parts.append(bx_ref[j, n] * gained)
        use(j, summed(parts))


def backward_kernel(
    s, w_ref, rhs_ref, rate_ref, skip_ref, damp_ref,
    gain_ref, bx_ref, cx_ref, total_ref, e_in, arrive_ref, sums_ref,
    e_out, out_ref, r_ref, tile_v,
):
    step = sums_ref[0] / sums_ref[1]

    def body(block, squares):
        tile_v[...] = rhs_ref[:, cols(block)]
        rates = load_rates(s, rate_ref, block)
        total = total_ref[block]
        before, after = totals_around(total)
        skip = spread(skip_ref[0:1, cols(block)])
        damp = spread(damp_ref[0:1, cols(block)])
        passed = enter(s, arrive_ref, e_in, block, rates, after)
        acc = [squares]

        def use(j, product):
            v = tile_v[pl.ds(j, SUB, stride=s.steps), :]
            r = v - step * (product + damp * v)
            r_ref[block, j] = r
            acc[0] = acc[0] + r * r

        backward_block(s, block, w_ref, skip, gain_ref, bx_ref, cx_ref, passed, use)

        def get_v(j):
            return r_ref[block, j]

        forward_summary(
            s, block, get_v, gain_ref, bx_ref, rates, total, e_out, out_ref
        )
        return acc[0]

    zero = jnp.zeros((SUB, LANE), F32)
    squares = lax.fori_loop(0, s.blocks, body, zero)
    put_sums(s, out_ref, squares, zero)


def last_kernel(
    s, w_ref, rhs_ref, r_ref, d_ref, rate_ref, skip_ref, damp_ref,
    gain_ref, bx_ref, cx_ref, total_ref, e_in, arrive_ref, sums_b, sums_c, sums_d,
    solution_ref, residual_ref, tile_v, tile_s, tile_r,
):
    before_step = sums_b[0] / sums_b[1]
    step = sums_c[0] / sums_d[1]

    def body(block, carry):
        tile_v[...] = rhs_ref[:, cols(block)]
        rates = load_rates(s, rate_ref, block)
        total = total_ref[block]
        before, after = totals_around(total)
        skip = spread(skip_ref[0:1, cols(block)])
        damp = spread(damp_ref[0:1, cols(block)])
        passed = enter(s, arrive_ref, e_in, block, rates, after)

        def use(j, product):
            rows = pl.ds(j, SUB, stride=s.steps)
            along = d_ref[block, j]
            tile_s[rows, :] = before_step * tile_v[rows, :] + step * along
            tile_r[rows, :] = r_ref[block, j] - step * (product + damp * along)

        backward_block(s, block, w_ref, skip, gain_ref, bx_ref, cx_ref, passed, use)
        solution_ref[:, cols(block)] = tile_s[...]
        residual_ref[:, cols(block)] = tile_r[...]
        return carry

    lax.fori_loop(0, s.blocks, body, 0)


VM = pl.BlockSpec(memory_space=pltpu.VMEM)
LIMIT = 4 * 1024 * 1024


def call(body, name, outs, scratch, args, limit=LIMIT):
    return pl.pallas_call(
        body,
        name=name,
        out_shape=outs,
        in_specs=[VM] * len(args),
        out_specs=[VM] * len(outs),
        scratch_shapes=scratch,
        compiler_params=pltpu.CompilerParams(vmem_limit_bytes=limit),
    )(*args)


def per_device(devices, rhs, rate, delta, b_proj, c_proj, skip, curvature, damping):
    tokens, columns = rhs.shape
    s = Sizes(tokens, columns, rate.shape[0], devices)
    skip, damping = skip[None], damping[None]
    held = pltpu.VMEM
    per_token = (s.blocks, s.steps, SUB, LANE)
    expanded = (s.steps, s.entries, SUB, LANE)
    edge = (s.blocks, s.entries, SUB, LANE)
    tile = pltpu.VMEM((tokens, LANE), F32)
    packet = jax.ShapeDtypeStruct((devices, 2 * s.rows, LANE), F32)

    def exchange(send):
        return lax.all_to_all(send, "seq", 0, 0)

    def link(got, decays, backward, has_sums, name):
        arrive, sums = call(
            functools.partial(link_kernel, s, backward, has_sums),
            name,
            [
                jax.ShapeDtypeStruct((devices, s.rows, LANE), F32),
                held((2, SUB, LANE), F32),
            ],
            [],
            (got, decays),
        )
        return exchange(arrive), sums

    gain, bx, cx, total, e, send = call(
        functools.partial(first_kernel, s),
        "first",
        [
            held((s.blocks, s.steps, s.entries, SUB, LANE), F32),
            held(expanded, F32),
            held(expanded, F32),
            held((s.blocks, SUB, LANE), F32),
            held(edge, F32),
            packet,
        ],
        [tile, tile],
        (rhs, delta, rate, b_proj, c_proj),
    )
    got_a = exchange(send)
    arrive, _ = link(got_a, got_a, False, False, "link_a")
    e, send, w, y0 = call(
        functools.partial(forward_kernel, s, True),
        "forward_a",
        [held(edge, F32), packet, held(per_token, F32), held(per_token, F32)],
        [tile, tile],
        (rhs, curvature, rate, skip, damping, gain, bx, cx, total, e, arrive),
    )
    arrive, sums_b = link(exchange(send), got_a, True, True, "link_b")
    e, send, r = call(
        functools.partial(backward_kernel, s),
        "backward_a",
        [held(edge, F32), packet, held(per_token, F32)],
        [tile],
        (w, rhs, rate, skip, damping, gain, bx, cx, total, e, arrive, sums_b),
    )
    arrive, sums_c = link(exchange(send), got_a, False, True, "link_c")
    e, send, w, d = call(
        functools.partial(forward_kernel, s, False),
        "forward_b",
        [held(edge, F32), packet, held(per_token, F32), held(per_token, F32)],
        [tile, tile],
        (
            r, curvature, rate, skip, damping, gain, bx, cx, total, e, arrive,
            rhs, y0, sums_b, sums_c,
        ),
    )
    arrive, sums_d = link(exchange(send), got_a, True, True, "link_d")
    whole = jax.ShapeDtypeStruct((tokens, columns), F32)
    return call(
        functools.partial(last_kernel, s),
        "backward_b",
        [whole, whole],
        [tile, tile, tile],
        (
            w, rhs, r, d, rate, skip, damping, gain, bx, cx, total, e, arrive,
            sums_b, sums_c, sums_d,
        ),
    )


def solution(mesh):
    placed = (
        P("seq", None),
        P(),
        P("seq", None),
        P("seq", None),
        P("seq", None),
        P(),
        P("seq", None),
        P(),
    )
    return jax.shard_map(
        functools.partial(per_device, mesh.shape["seq"]),
        mesh=mesh,
        in_specs=placed,
        out_specs=(P("seq", None), P("seq", None)),
        check_vma=False,
    )
```

```python
import functools

import jax
import jax.numpy as jnp
from jax import lax
from jax.experimental import pallas as pl
from jax.experimental.pallas import tpu as pltpu
from jax.sharding import PartitionSpec as P

STREAMS = 1
SUB, LANE = 8, 128
LOG2E = 1.4426950408889634
LN2 = 0.6931471805599453
SMALL = 0.03
G1, G2, G3 = -LN2, -LN2 * LN2 / 2.0, -LN2 * LN2 * LN2 / 6.0
F32 = jnp.float32


def sub_index():
    return lax.broadcasted_iota(jnp.int32, (SUB, LANE), 0)


def spread(row):
    return jnp.broadcast_to(row, (SUB, LANE))


def rolled(x, shift):
    return pltpu.roll(x, shift % SUB, 0)


def scan_chunks(value, decay, backward):
    at = sub_index()
    edge = at == (SUB - 1 if backward else 0)
    keep = jnp.where(edge, 0.0, decay)
    for step in (1, 2, 4):
        shift = -step if backward else step
        value = value + keep * rolled(value, shift)
        if step < 4:
            keep = keep * rolled(keep, shift)
    entering = jnp.where(edge, 0.0, rolled(value, -1 if backward else 1))
    last = value[0:1] if backward else value[SUB - 1 : SUB]
    return entering, last


def total_around(total, backward):
    at = sub_index()
    edge = at == (SUB - 1 if backward else 0)
    side = -1 if backward else 1
    value = jnp.where(edge, 0.0, rolled(total, side))
    for step in (1, 2, 4):
        inside = at < SUB - step if backward else at >= step
        value = value + jnp.where(inside, rolled(value, side * step), 0.0)
    return value


def summed(parts):
    while len(parts) > 1:
        parts = [sum(parts[i : i + 2]) for i in range(0, len(parts), 2)]
    return parts[0]


class Sizes:
    def __init__(self, tokens, columns, entries, devices, streams):
        self.tokens, self.entries, self.devices = tokens, entries, devices
        self.steps = tokens // SUB
        self.blocks = columns // LANE // streams
        self.rows = entries * self.blocks // devices
        self.per = entries // self.rows


def cols(block):
    return pl.ds(pl.multiple_of(block * LANE, LANE), LANE)


def lane_row(row):
    return pl.ds(row * LANE, LANE)


def write_state(s, ref, block, rows_of):
    for n, value in enumerate(rows_of):
        ref[block * s.per + n // s.rows, 0:1, lane_row(n % s.rows)] = value


def read_state(s, ref, block):
    return [
        spread(ref[block * s.per + n // s.rows, 0:1, lane_row(n % s.rows)])
        for n in range(s.entries)
    ]


def load_rates(s, rate_ref, block):
    return [spread(rate_ref[n : n + 1, cols(block)]) for n in range(s.entries)]


def finish_summary(s, block, state, rates, total, e_ref, put, backward):
    lasts = []
    for n in range(s.entries):
        entering, last = scan_chunks(state[n], jnp.exp2(total * rates[n]), backward)
        e_ref[block, n] = entering
        lasts.append(last)
    write_state(s, put, block, lasts)


def zeros(count):
    return [jnp.zeros((SUB, LANE), F32)] * count


def first_kernel(s, offset, *refs):
    rhs_hbm, delta_hbm, curv_hbm, rate_hbm, skip_hbm, damp_hbm, bt_hbm, ct_hbm = refs[:8]
    (
        decay_ref, drive_ref, cx_ref, total_ref, e_ref, out_ref,
        rhs_ref, curv_ref, rate_ref, skip_ref, damp_ref, link_rate_ref,
    ) = refs[8:20]
    delta_ref, bx_ref, wide_ref, turn_ref, sem_d, sem_v, sem_c, sem_s = refs[20:]

    small = [
        pltpu.make_async_copy(src, dst, sem_s.at[i])
        for i, (src, dst) in enumerate(
            [
                (bt_hbm, wide_ref.at[0]), (ct_hbm, wide_ref.at[1]), (rate_hbm, rate_ref),
                (skip_hbm, skip_ref), (damp_hbm, damp_ref),
            ]
        )
    ]

    def block_copy(src, dst, sem, block):
        return pltpu.make_async_copy(
            src.at[:, cols(block + offset)], dst.at[block], sem.at[block]
        )

    for copy in small[:3]:
        copy.start()
    for block in range(s.blocks):
        block_copy(delta_hbm, delta_ref, sem_d, block).start()
        block_copy(rhs_hbm, rhs_ref, sem_v, block).start()
    for copy in small[3:]:
        copy.start()
    for block in range(s.blocks):
        block_copy(curv_hbm, curv_ref, sem_c, block).start()

    for index, dst in enumerate([bx_ref, cx_ref]):
        small[index].wait()
        turn_ref[index] = jnp.transpose(wide_ref[index])
        for j in range(s.steps):
            turned = turn_ref[index, pl.ds(j, SUB, stride=s.steps), :]
            for n in range(s.entries):
                dst[j, n] = jnp.broadcast_to(turned[:, n : n + 1], (SUB, LANE))
    small[2].wait()
    rate_ref[...] = rate_ref[...] * (-LOG2E)

    def body(block, carry):
        block_copy(delta_hbm, delta_ref, sem_d, block).wait()
        block_copy(rhs_hbm, rhs_ref, sem_v, block).wait()
        own = [rate_ref[n : n + 1, cols(block + offset)] for n in range(s.entries)]
        write_state(s, link_rate_ref, block, own)
        rates = [spread(row) for row in own]

        def advance(j, state):
            total, state = state[0], list(state[1:])
            rows = pl.ds(j, SUB, stride=s.steps)
            d = delta_ref[block, rows, :]
            v = rhs_ref[block, rows, :]
            total = total + d
            for n in range(s.entries):
                z = d * rates[n]
                decay = jnp.exp2(z)
                near = z * (G1 + z * (G2 + z * G3))
                drive = jnp.where(z > -SMALL, near, 1.0 - decay) * bx_ref[j, n]
                decay_ref[block, j, n] = decay
                drive_ref[block, j, n] = drive
                state[n] = decay * state[n] + drive * v
            return (total, *state)

        result = lax.fori_loop(0, s.steps, advance, tuple(zeros(s.entries + 1)), unroll=8)
        total, state = result[0], result[1:]
        total_ref[block] = total
        finish_summary(s, block, state, rates, total, e_ref, out_ref, False)
        whole = jnp.sum(total, axis=0, keepdims=True)
        for piece in range(s.per):
            out_ref[block * s.per + piece, 0:1, lane_row(s.rows)] = whole
        return carry

    lax.fori_loop(0, s.blocks, body, 0)
    small[3].wait()
    small[4].wait()

    def finish(block, carry):
        block_copy(curv_hbm, curv_ref, sem_c, block).wait()
        return carry

    lax.fori_loop(0, s.blocks, finish, 0)


def put_sums(s, out_ref, first, second):
    first = jnp.sum(first, axis=0, keepdims=True)
    second = jnp.sum(second, axis=0, keepdims=True)
    half = LANE // 2
    first = first + pltpu.roll(first, half, 1)
    second = second + pltpu.roll(second, half, 1)
    lane = lax.broadcasted_iota(jnp.int32, (1, LANE), 1)
    both = jnp.where(lane < half, first, second)

    def body(device, carry):
        out_ref[device, 0:1, lane_row(s.rows)] = both
        return carry

    lax.fori_loop(0, s.devices, body, 0, unroll=8)


def link_kernel(s, backward, first, *refs):
    if first:
        got_ref, link_rate_ref, arrive_ref, decay_ref = refs
        rates = link_rate_ref[lax.axis_index("seq")]
    else:
        got_ref, decay_ref, arrive_ref, sums_ref = refs
    wide = s.rows * LANE
    carried = jnp.zeros((1, wide), F32)
    tail = jnp.zeros((1, LANE), F32)
    order = range(s.devices)
    for device in reversed(order) if backward else order:
        extra = got_ref[device, :, lane_row(s.rows)]
        if first:
            decay = jnp.exp2(jnp.concatenate([extra] * s.rows, axis=1) * rates)
            decay_ref[device] = decay
        else:
            decay = decay_ref[device]
            tail = tail + extra
        arrive_ref[device] = carried
        carried = decay * carried + got_ref[device, :, 0:wide]
    if not first:
        lane = lax.broadcasted_iota(jnp.int32, (1, LANE), 1)
        low = jnp.where(lane < LANE // 2, tail, 0.0)
        high = jnp.where(lane < LANE // 2, 0.0, tail)
        sums_ref[0] = spread(jnp.sum(low, axis=1, keepdims=True))
        sums_ref[1] = spread(jnp.sum(high, axis=1, keepdims=True))


def total_sum(sums, index):
    return sum(ref[index] for ref in sums)


def enter(s, arrive_ref, e_ref, block, rates, around):
    arrive = read_state(s, arrive_ref, block)
    return [
        e_ref[block, n] + jnp.exp2(around * rates[n]) * arrive[n]
        for n in range(s.entries)
    ]


def forward_kernel(s, offset, first, *refs):
    refs = list(refs)
    rhs_ref, curv_ref, rate_ref, skip_ref, damp_ref = refs[:5]
    decay_ref, drive_ref, cx_ref, total_ref, e_in, arrive_ref = refs[5:11]
    refs = refs[11:]
    if not first:
        r_ref, y0_ref = refs[:2]
        sums_b, sums_c = refs[2 : 2 + STREAMS], refs[2 + STREAMS : 2 + 2 * STREAMS]
        refs = refs[2 + 2 * STREAMS :]
        ratio = total_sum(sums_c, 0) / total_sum(sums_b, 0)
    e_out, out_ref, w_ref, y_ref = refs

    def body(block, carry):
        squares, inner = carry
        rates = load_rates(s, rate_ref, block + offset)
        total = total_ref[block]
        skip = spread(skip_ref[0:1, cols(block + offset)])
        damp = spread(damp_ref[0:1, cols(block + offset)])
        before = total_around(total, False)
        state = enter(s, arrive_ref, e_in, block, rates, before)
        for j in range(s.steps):
            rows = pl.ds(j, SUB, stride=s.steps)
            rhs = rhs_ref[block, rows, :]
            v = rhs if first else r_ref[block, j]
            parts = [skip * v]
            for n in range(s.entries):
                state[n] = (
                    decay_ref[block, j, n] * state[n] + drive_ref[block, j, n] * v
                )
                parts.append(cx_ref[j, n] * state[n])
            y = summed(parts)
            if first:
                y_ref[block, j] = y
                squares = squares + v * v
                along = v
            else:
                y = y + ratio * y0_ref[block, j]
                along = v + ratio * rhs
                y_ref[block, j] = along
            w = curv_ref[block, rows, :] * y
            w_ref[block, j] = w
            inner = inner + (w * y + damp * (along * along))

        passed = zeros(s.entries)
        for j in reversed(range(s.steps)):
            w = w_ref[block, j]
            for n in range(s.entries):
                passed[n] = decay_ref[block, j, n] * (cx_ref[j, n] * w + passed[n])
        finish_summary(s, block, passed, rates, total, e_out, out_ref, True)
        return squares, inner

    squares, inner = lax.fori_loop(0, s.blocks, body, tuple(zeros(2)))
    put_sums(s, out_ref, squares, inner)


def backward_block(s, block, w_ref, skip, decay_ref, drive_ref, cx_ref, passed, use):
    for j in reversed(range(s.steps)):
        w = w_ref[block, j]
        parts = [skip * w]
        for n in range(s.entries):
            costate = cx_ref[j, n] * w + passed[n]
            passed[n] = decay_ref[block, j, n] * costate
            parts.append(drive_ref[block, j, n] * costate)
        use(j, summed(parts))


def backward_kernel(s, offset, *refs):
    rhs_ref, rate_ref, skip_ref, damp_ref = refs[:4]
    decay_ref, drive_ref, cx_ref, total_ref, e_in, arrive_ref, w_ref = refs[4:11]
    sums_b = refs[11 : 11 + STREAMS]
    e_out, out_ref, r_ref = refs[11 + STREAMS :]
    step = total_sum(sums_b, 0) / total_sum(sums_b, 1)

    def body(block, squares):
        rates = load_rates(s, rate_ref, block + offset)
        total = total_ref[block]
        skip = spread(skip_ref[0:1, cols(block + offset)])
        damp = spread(damp_ref[0:1, cols(block + offset)])
        after = total_around(total, True)
        passed = enter(s, arrive_ref, e_in, block, rates, after)
        acc = [squares]

        def use(j, product):
            v = rhs_ref[block, pl.ds(j, SUB, stride=s.steps), :]
            r = v - step * (product + damp * v)
            r_ref[block, j] = r
            acc[0] = acc[0] + r * r

        backward_block(
            s, block, w_ref, skip, decay_ref, drive_ref, cx_ref, passed, use
        )
        state = zeros(s.entries)
        for j in range(s.steps):
            v = r_ref[block, j]
            for n in range(s.entries):
                state[n] = (
                    decay_ref[block, j, n] * state[n] + drive_ref[block, j, n] * v
                )
        finish_summary(s, block, state, rates, total, e_out, out_ref, False)
        return acc[0]

    squares = lax.fori_loop(0, s.blocks, body, zeros(1)[0])
    put_sums(s, out_ref, squares, zeros(1)[0])


def last_kernel(s, offset, *refs):
    rhs_ref, rate_ref, skip_ref, damp_ref = refs[:4]
    decay_ref, drive_ref, cx_ref, total_ref, e_in, arrive_ref, w_ref = refs[4:11]
    r_ref, d_ref = refs[11:13]
    refs = refs[13:]
    sums_b, sums_c = refs[:STREAMS], refs[STREAMS : 2 * STREAMS]
    sums_d = refs[2 * STREAMS : 3 * STREAMS]
    refs = refs[3 * STREAMS :]
    if offset:
        refs = refs[2:]
    solution_ref, residual_ref, tile_s, tile_r, sem_s, sem_r = refs
    before_step = total_sum(sums_b, 0) / total_sum(sums_b, 1)
    step = total_sum(sums_c, 0) / total_sum(sums_d, 1)

    def copies(block):
        where = cols(block + offset)
        return (
            pltpu.make_async_copy(
                tile_s.at[block], solution_ref.at[:, where], sem_s.at[block]
            ),
            pltpu.make_async_copy(
                tile_r.at[block], residual_ref.at[:, where], sem_r.at[block]
            ),
        )

    def body(block, carry):
        rates = load_rates(s, rate_ref, block + offset)
        skip = spread(skip_ref[0:1, cols(block + offset)])
        damp = spread(damp_ref[0:1, cols(block + offset)])
        after = total_around(total_ref[block], True)
        passed = enter(s, arrive_ref, e_in, block, rates, after)

        def use(j, product):
            rows = pl.ds(j, SUB, stride=s.steps)
            along = d_ref[block, j]
            tile_s[block, rows, :] = (
                before_step * rhs_ref[block, rows, :] + step * along
            )
            tile_r[block, rows, :] = r_ref[block, j] - step * (product + damp * along)

        backward_block(
            s, block, w_ref, skip, decay_ref, drive_ref, cx_ref, passed, use
        )
        for copy in copies(block):
            copy.start()
        return carry

    lax.fori_loop(0, s.blocks, body, 0)

    def finish(block, carry):
        for copy in copies(block):
            copy.wait()
        return carry

    lax.fori_loop(0, s.blocks, finish, 0)


VM = pl.BlockSpec(memory_space=pltpu.VMEM)
HBM = pl.BlockSpec(memory_space=pltpu.HBM)
LIMIT = 4 * 1024 * 1024


def in_hbm(x):
    return pltpu.with_memory_space_constraint(x, pltpu.HBM)


def call(body, name, outs, scratch, args, passes, n_hbm=0, out_specs=None, aliases=()):
    work = passes * 16 * 128 * 2048 // STREAMS
    return pl.pallas_call(
        body,
        name=name,
        out_shape=outs,
        in_specs=[HBM] * n_hbm + [VM] * (len(args) - n_hbm),
        out_specs=out_specs or [VM] * len(outs),
        scratch_shapes=scratch,
        input_output_aliases=dict(aliases),
        cost_estimate=pl.CostEstimate(
            flops=work, bytes_accessed=work, transcendentals=0
        ),
        compiler_params=pltpu.CompilerParams(vmem_limit_bytes=LIMIT),
    )(*args)


def per_device(devices, rhs, rate, delta, b_proj, c_proj, skip, curvature, damping):
    tokens, columns = rhs.shape
    entries = rate.shape[0]
    s = Sizes(tokens, columns, entries, devices, STREAMS)
    held = pltpu.VMEM
    dma = pltpu.SemaphoreType.DMA
    every = range(STREAMS)
    per_token = held((s.blocks, s.steps, SUB, LANE), F32)
    expanded = (s.steps, entries, SUB, LANE)
    edge = held((s.blocks, entries, SUB, LANE), F32)
    whole_state = held((s.blocks, s.steps, entries, SUB, LANE), F32)
    tile = (s.blocks, tokens, LANE)
    packet = held((devices, 1, (s.rows + 1) * LANE), F32)
    linked = held((devices, 1, s.rows * LANE), F32)
    sums = held((2, SUB, LANE), F32)

    def exchange(send):
        return lax.all_to_all(send, "seq", 0, 0)

    def kernel(body, *more):
        return functools.partial(body, s, *more)

    offsets = [s.blocks * g for g in every]
    firsts = [
        call(
            kernel(first_kernel, offsets[g]),
            f"first_{g}",
            [
                whole_state, whole_state, held(expanded, F32),
                held((s.blocks, SUB, LANE), F32), edge, packet,
                held(tile, F32), held(tile, F32), held((entries, columns), F32),
                held((1, columns), F32), held((1, columns), F32), linked,
            ],
            [
                pltpu.VMEM(tile, F32), pltpu.VMEM(expanded, F32),
                pltpu.VMEM((2, entries, tokens), F32),
                pltpu.VMEM((2, tokens, entries), F32),
                dma((s.blocks,)), dma((s.blocks,)), dma((s.blocks,)), dma((5,)),
            ],
            [
                in_hbm(x)
                for x in (
                    rhs, delta, curvature, rate, skip[None], damping[None],
                    b_proj.T, c_proj.T,
                )
            ],
            2,
            n_hbm=8,
        )
        for g in every
    ]
    decay, drive, cx, total, e, send, rhs_v, curv, rates, skips, damps, link_rate = zip(
        *firsts
    )

    def link(g, got, backward, letter, decays=None):
        first = decays is None
        return call(
            kernel(link_kernel, backward, first),
            f"link_{letter}_{g}",
            [linked, linked if first else sums],
            [],
            (got, link_rate[g] if first else decays),
            1,
        )

    def around(send, backward, letter, decays):
        got = [exchange(send[g]) for g in every]
        pairs = [link(g, got[g], backward, letter, decays and decays[g]) for g in every]
        return [exchange(pairs[g][0]) for g in every], [pairs[g][1] for g in every]

    def common(g, e, arrive):
        return (decay[g], drive[g], cx[g], total[g], e[g], arrive[g])

    def consts(g):
        return (rates[g], skips[g], damps[g])

    arrive, decays = around(send, False, "a", None)
    e, send, w, y0 = zip(
        *[
            call(
                kernel(forward_kernel, offsets[g], True),
                f"forward_a_{g}",
                [edge, packet, per_token, per_token],
                [],
                (rhs_v[g], curv[g], *consts(g), *common(g, e, arrive)),
                2,
            )
            for g in every
        ]
    )
    arrive, sums_b = around(send, True, "b", decays)
    e, send, r = zip(
        *[
            call(
                kernel(backward_kernel, offsets[g]),
                f"backward_a_{g}",
                [edge, packet, per_token],
                [],
                (rhs_v[g], *consts(g), *common(g, e, arrive), w[g], *sums_b),
                2,
            )
            for g in every
        ]
    )
    arrive, sums_c = around(send, False, "c", decays)
    e, send, w, d = zip(
        *[
            call(
                kernel(forward_kernel, offsets[g], False),
                f"forward_b_{g}",
                [edge, packet, per_token, per_token],
                [],
                (
                    rhs_v[g], curv[g], *consts(g), *common(g, e, arrive),
                    r[g], y0[g], *sums_b, *sums_c,
                ),
                2,
            )
            for g in every
        ]
    )
    arrive, sums_d = around(send, True, "d", decays)
    outs = ()
    for g in every:
        args = (
            rhs_v[g], *consts(g), *common(g, e, arrive), w[g], r[g], d[g],
            *sums_b, *sums_c, *sums_d,
        )
        outs = pl.pallas_call(
            kernel(last_kernel, offsets[g]),
            name=f"backward_b_{g}",
            out_shape=[jax.ShapeDtypeStruct((tokens, columns), F32)] * 2,
            in_specs=[VM] * len(args) + [HBM] * len(outs),
            out_specs=[HBM] * 2,
            scratch_shapes=[
                pltpu.VMEM(tile, F32), pltpu.VMEM(tile, F32),
                dma((s.blocks,)), dma((s.blocks,)),
            ],
            input_output_aliases={len(args): 0, len(args) + 1: 1} if outs else {},
            compiler_params=pltpu.CompilerParams(vmem_limit_bytes=LIMIT),
        )(*args, *outs)
    return tuple(outs)


def solution(mesh):
    placed = (
        P("seq", None),
        P(),
        P("seq", None),
        P("seq", None),
        P("seq", None),
        P(),
        P("seq", None),
        P(),
    )
    return jax.shard_map(
        functools.partial(per_device, mesh.shape["seq"]),
        mesh=mesh,
        in_specs=placed,
        out_specs=(P("seq", None), P("seq", None)),
        check_vma=False,
    )
```

```python
import functools

import jax
import jax.numpy as jnp
from jax import lax
from jax.experimental import pallas as pl
from jax.experimental.pallas import tpu as pltpu
from jax.sharding import PartitionSpec as P

STREAMS = 1
SUB, LANE = 8, 128
LOG2E = 1.4426950408889634
HALF = -0.5 * 0.6931471805599453
F32 = jnp.float32


def sub_index():
    return lax.broadcasted_iota(jnp.int32, (SUB, LANE), 0)


def spread(row):
    return jnp.broadcast_to(row, (SUB, LANE))


def rolled(x, shift):
    return pltpu.roll(x, shift % SUB, 0)


def scan_chunks(value, decay, backward):
    at = sub_index()
    edge = at == (SUB - 1 if backward else 0)
    keep = jnp.where(edge, 0.0, decay)
    for step in (1, 2, 4):
        shift = -step if backward else step
        value = value + keep * rolled(value, shift)
        if step < 4:
            keep = keep * rolled(keep, shift)
    entering = jnp.where(edge, 0.0, rolled(value, -1 if backward else 1))
    last = value[0:1] if backward else value[SUB - 1 : SUB]
    return entering, last


def total_around(total, backward):
    at = sub_index()
    edge = at == (SUB - 1 if backward else 0)
    side = -1 if backward else 1
    value = jnp.where(edge, 0.0, rolled(total, side))
    for step in (1, 2, 4):
        inside = at < SUB - step if backward else at >= step
        value = value + jnp.where(inside, rolled(value, side * step), 0.0)
    return value


def summed(parts):
    while len(parts) > 1:
        parts = [sum(parts[i : i + 2]) for i in range(0, len(parts), 2)]
    return parts[0]


class Sizes:
    def __init__(self, tokens, columns, entries, devices, streams):
        self.tokens, self.entries, self.devices = tokens, entries, devices
        self.steps = tokens // SUB
        self.blocks = columns // LANE // streams
        self.rows = entries * self.blocks // devices
        self.per = entries // self.rows


def cols(block):
    return pl.ds(pl.multiple_of(block * LANE, LANE), LANE)


def lane_row(row):
    return pl.ds(row * LANE, LANE)


def write_state(s, ref, block, rows_of):
    for n, value in enumerate(rows_of):
        ref[block * s.per + n // s.rows, 0:1, lane_row(n % s.rows)] = value


def read_state(s, ref, block):
    return [
        spread(ref[block * s.per + n // s.rows, 0:1, lane_row(n % s.rows)])
        for n in range(s.entries)
    ]


def load_rates(s, rate_ref, block):
    return [spread(rate_ref[n : n + 1, cols(block)]) for n in range(s.entries)]


def finish_summary(s, block, state, rates, total, e_ref, put, backward):
    lasts = []
    for n in range(s.entries):
        entering, last = scan_chunks(state[n], jnp.exp2(total * rates[n]), backward)
        e_ref[block, n] = entering
        lasts.append(last)
    write_state(s, put, block, lasts)


def zeros(count):
    return [jnp.zeros((SUB, LANE), F32)] * count


def first_kernel(s, offset, *refs):
    rhs_hbm, delta_hbm, curv_hbm, rate_hbm, skip_hbm, damp_hbm, bt_hbm, ct_hbm = refs[:8]
    (
        decay_ref, drive_ref, cx_ref, total_ref, e_ref, out_ref,
        rhs_ref, curv_ref, rate_ref, skip_ref, damp_ref, link_rate_ref,
    ) = refs[8:20]
    delta_ref, bx_ref, wide_ref, turn_ref, sem_d, sem_v, sem_c, sem_s = refs[20:]

    small = [
        pltpu.make_async_copy(src, dst, sem_s.at[i])
        for i, (src, dst) in enumerate(
            [
                (bt_hbm, wide_ref.at[0]), (ct_hbm, wide_ref.at[1]), (rate_hbm, rate_ref),
                (skip_hbm, skip_ref), (damp_hbm, damp_ref),
            ]
        )
    ]

    def block_copy(src, dst, sem, block):
        return pltpu.make_async_copy(
            src.at[:, cols(block + offset)], dst.at[block], sem.at[block]
        )

    for copy in small[:3]:
        copy.start()
    for block in range(s.blocks):
        block_copy(delta_hbm, delta_ref, sem_d, block).start()
        block_copy(rhs_hbm, rhs_ref, sem_v, block).start()
    for copy in small[3:]:
        copy.start()
    for block in range(s.blocks):
        block_copy(curv_hbm, curv_ref, sem_c, block).start()

    for index, dst in enumerate([bx_ref, cx_ref]):
        small[index].wait()
        turn_ref[index] = jnp.transpose(wide_ref[index])
        for j in range(s.steps):
            turned = turn_ref[index, pl.ds(j, SUB, stride=s.steps), :]
            for n in range(s.entries):
                dst[j, n] = jnp.broadcast_to(turned[:, n : n + 1], (SUB, LANE))
    small[2].wait()
    rate_ref[...] = rate_ref[...] * (-LOG2E)

    def body(block, carry):
        block_copy(delta_hbm, delta_ref, sem_d, block).wait()
        block_copy(rhs_hbm, rhs_ref, sem_v, block).wait()
        own = [rate_ref[n : n + 1, cols(block + offset)] for n in range(s.entries)]
        write_state(s, link_rate_ref, block, own)
        rates = [spread(row) for row in own]

        def advance(j, state):
            total, state = state[0], list(state[1:])
            rows = pl.ds(j, SUB, stride=s.steps)
            d = delta_ref[block, rows, :]
            v = rhs_ref[block, rows, :]
            total = total + d
            for n in range(s.entries):
                z = d * rates[n]
                decay = jnp.exp2(z)
                drive = jnp.tanh(z * HALF) * (bx_ref[j, n] * (1.0 + decay))
                decay_ref[block, j, n] = decay
                drive_ref[block, j, n] = drive
                state[n] = decay * state[n] + drive * v
            return (total, *state)

        result = lax.fori_loop(0, s.steps, advance, tuple(zeros(s.entries + 1)), unroll=16)
        total, state = result[0], result[1:]
        total_ref[block] = total
        finish_summary(s, block, state, rates, total, e_ref, out_ref, False)
        whole = jnp.sum(total, axis=0, keepdims=True)
        for piece in range(s.per):
            out_ref[block * s.per + piece, 0:1, lane_row(s.rows)] = whole
        return carry

    lax.fori_loop(0, s.blocks, body, 0)
    small[3].wait()
    small[4].wait()

    def finish(block, carry):
        block_copy(curv_hbm, curv_ref, sem_c, block).wait()
        return carry

    lax.fori_loop(0, s.blocks, finish, 0)


def put_sums(s, out_ref, first, second):
    first = jnp.sum(first, axis=0, keepdims=True)
    second = jnp.sum(second, axis=0, keepdims=True)
    half = LANE // 2
    first = first + pltpu.roll(first, half, 1)
    second = second + pltpu.roll(second, half, 1)
    lane = lax.broadcasted_iota(jnp.int32, (1, LANE), 1)
    both = jnp.where(lane < half, first, second)

    def body(device, carry):
        out_ref[device, 0:1, lane_row(s.rows)] = both
        return carry

    lax.fori_loop(0, s.devices, body, 0, unroll=8)


def link_kernel(s, backward, first, *refs):
    if first:
        got_ref, link_rate_ref, arrive_ref, decay_ref = refs
        rates = link_rate_ref[lax.axis_index("seq")]
    else:
        got_ref, decay_ref, arrive_ref, sums_ref = refs
    wide = s.rows * LANE
    carried = jnp.zeros((1, wide), F32)
    tail = jnp.zeros((1, LANE), F32)
    order = range(s.devices)
    for device in reversed(order) if backward else order:
        extra = got_ref[device, :, lane_row(s.rows)]
        if first:
            decay = jnp.exp2(jnp.concatenate([extra] * s.rows, axis=1) * rates)
            decay_ref[device] = decay
        else:
            decay = decay_ref[device]
            tail = tail + extra
        arrive_ref[device] = carried
        carried = decay * carried + got_ref[device, :, 0:wide]
    if not first:
        lane = lax.broadcasted_iota(jnp.int32, (1, LANE), 1)
        low = jnp.where(lane < LANE // 2, tail, 0.0)
        high = jnp.where(lane < LANE // 2, 0.0, tail)
        sums_ref[0] = spread(jnp.sum(low, axis=1, keepdims=True))
        sums_ref[1] = spread(jnp.sum(high, axis=1, keepdims=True))


def total_sum(sums, index):
    return sum(ref[index] for ref in sums)


def enter(s, arrive_ref, e_ref, block, rates, around):
    arrive = read_state(s, arrive_ref, block)
    return [
        e_ref[block, n] + jnp.exp2(around * rates[n]) * arrive[n]
        for n in range(s.entries)
    ]


def forward_kernel(s, offset, first, *refs):
    refs = list(refs)
    rhs_ref, curv_ref, rate_ref, skip_ref, damp_ref = refs[:5]
    decay_ref, drive_ref, cx_ref, total_ref, e_in, arrive_ref = refs[5:11]
    refs = refs[11:]
    if not first:
        r_ref, y0_ref = refs[:2]
        sums_b, sums_c = refs[2 : 2 + STREAMS], refs[2 + STREAMS : 2 + 2 * STREAMS]
        refs = refs[2 + 2 * STREAMS :]
        ratio = total_sum(sums_c, 0) / total_sum(sums_b, 0)
    e_out, out_ref, w_ref, y_ref = refs

    def body(block, carry):
        squares, inner = carry
        rates = load_rates(s, rate_ref, block + offset)
        total = total_ref[block]
        skip = spread(skip_ref[0:1, cols(block + offset)])
        damp = spread(damp_ref[0:1, cols(block + offset)])
        before = total_around(total, False)
        state = enter(s, arrive_ref, e_in, block, rates, before)
        for j in range(s.steps):
            rows = pl.ds(j, SUB, stride=s.steps)
            rhs = rhs_ref[block, rows, :]
            v = rhs if first else r_ref[block, j]
            parts = [skip * v]
            for n in range(s.entries):
                state[n] = (
                    decay_ref[block, j, n] * state[n] + drive_ref[block, j, n] * v
                )
                parts.append(cx_ref[j, n] * state[n])
            y = summed(parts)
            if first:
                y_ref[block, j] = y
                squares = squares + v * v
                along = v
            else:
                y = y + ratio * y0_ref[block, j]
                along = v + ratio * rhs
                y_ref[block, j] = along
            w = curv_ref[block, rows, :] * y
            w_ref[block, j] = w
            inner = inner + (w * y + damp * (along * along))

        passed = zeros(s.entries)
        for j in reversed(range(s.steps)):
            w = w_ref[block, j]
            for n in range(s.entries):
                passed[n] = decay_ref[block, j, n] * (cx_ref[j, n] * w + passed[n])
        finish_summary(s, block, passed, rates, total, e_out, out_ref, True)
        return squares, inner

    squares, inner = lax.fori_loop(0, s.blocks, body, tuple(zeros(2)))
    put_sums(s, out_ref, squares, inner)


def backward_block(s, block, w_ref, skip, decay_ref, drive_ref, cx_ref, passed, use):
    for j in reversed(range(s.steps)):
        w = w_ref[block, j]
        parts = [skip * w]
        for n in range(s.entries):
            costate = cx_ref[j, n] * w + passed[n]
            passed[n] = decay_ref[block, j, n] * costate
            parts.append(drive_ref[block, j, n] * costate)
        use(j, summed(parts))


def backward_kernel(s, offset, *refs):
    rhs_ref, rate_ref, skip_ref, damp_ref = refs[:4]
    decay_ref, drive_ref, cx_ref, total_ref, e_in, arrive_ref, w_ref = refs[4:11]
    sums_b = refs[11 : 11 + STREAMS]
    e_out, out_ref, r_ref = refs[11 + STREAMS :]
    step = total_sum(sums_b, 0) / total_sum(sums_b, 1)

    def body(block, squares):
        rates = load_rates(s, rate_ref, block + offset)
        total = total_ref[block]
        skip = spread(skip_ref[0:1, cols(block + offset)])
        damp = spread(damp_ref[0:1, cols(block + offset)])
        after = total_around(total, True)
        passed = enter(s, arrive_ref, e_in, block, rates, after)
        acc = [squares]

        def use(j, product):
            v = rhs_ref[block, pl.ds(j, SUB, stride=s.steps), :]
            r = v - step * (product + damp * v)
            r_ref[block, j] = r
            acc[0] = acc[0] + r * r

        backward_block(
            s, block, w_ref, skip, decay_ref, drive_ref, cx_ref, passed, use
        )
        state = zeros(s.entries)
        for j in range(s.steps):
            v = r_ref[block, j]
            for n in range(s.entries):
                state[n] = (
                    decay_ref[block, j, n] * state[n] + drive_ref[block, j, n] * v
                )
        finish_summary(s, block, state, rates, total, e_out, out_ref, False)
        return acc[0]

    squares = lax.fori_loop(0, s.blocks, body, zeros(1)[0])
    put_sums(s, out_ref, squares, zeros(1)[0])


def last_kernel(s, offset, *refs):
    rhs_ref, rate_ref, skip_ref, damp_ref = refs[:4]
    decay_ref, drive_ref, cx_ref, total_ref, e_in, arrive_ref, w_ref = refs[4:11]
    r_ref, d_ref = refs[11:13]
    refs = refs[13:]
    sums_b, sums_c = refs[:STREAMS], refs[STREAMS : 2 * STREAMS]
    sums_d = refs[2 * STREAMS : 3 * STREAMS]
    refs = refs[3 * STREAMS :]
    if offset:
        refs = refs[2:]
    solution_ref, residual_ref, tile_s, tile_r, sem_s, sem_r = refs
    before_step = total_sum(sums_b, 0) / total_sum(sums_b, 1)
    step = total_sum(sums_c, 0) / total_sum(sums_d, 1)

    def copies(block):
        where = cols(block + offset)
        return (
            pltpu.make_async_copy(
                tile_s.at[block], solution_ref.at[:, where], sem_s.at[block]
            ),
            pltpu.make_async_copy(
                tile_r.at[block], residual_ref.at[:, where], sem_r.at[block]
            ),
        )

    def body(block, carry):
        rates = load_rates(s, rate_ref, block + offset)
        skip = spread(skip_ref[0:1, cols(block + offset)])
        damp = spread(damp_ref[0:1, cols(block + offset)])
        after = total_around(total_ref[block], True)
        passed = enter(s, arrive_ref, e_in, block, rates, after)

        def use(j, product):
            rows = pl.ds(j, SUB, stride=s.steps)
            along = d_ref[block, j]
            tile_s[block, rows, :] = (
                before_step * rhs_ref[block, rows, :] + step * along
            )
            tile_r[block, rows, :] = r_ref[block, j] - step * (product + damp * along)

        backward_block(
            s, block, w_ref, skip, decay_ref, drive_ref, cx_ref, passed, use
        )
        for copy in copies(block):
            copy.start()
        return carry

    lax.fori_loop(0, s.blocks, body, 0)

    def finish(block, carry):
        for copy in copies(block):
            copy.wait()
        return carry

    lax.fori_loop(0, s.blocks, finish, 0)


VM = pl.BlockSpec(memory_space=pltpu.VMEM)
HBM = pl.BlockSpec(memory_space=pltpu.HBM)
LIMIT = 4 * 1024 * 1024


def in_hbm(x):
    return pltpu.with_memory_space_constraint(x, pltpu.HBM)


def call(body, name, outs, scratch, args, passes, n_hbm=0, out_specs=None, aliases=()):
    work = passes * 16 * 128 * 2048 // STREAMS
    return pl.pallas_call(
        body,
        name=name,
        out_shape=outs,
        in_specs=[HBM] * n_hbm + [VM] * (len(args) - n_hbm),
        out_specs=out_specs or [VM] * len(outs),
        scratch_shapes=scratch,
        input_output_aliases=dict(aliases),
        cost_estimate=pl.CostEstimate(
            flops=work, bytes_accessed=work, transcendentals=0
        ),
        compiler_params=pltpu.CompilerParams(vmem_limit_bytes=LIMIT),
    )(*args)


def per_device(devices, rhs, rate, delta, b_proj, c_proj, skip, curvature, damping):
    tokens, columns = rhs.shape
    entries = rate.shape[0]
    s = Sizes(tokens, columns, entries, devices, STREAMS)
    held = pltpu.VMEM
    dma = pltpu.SemaphoreType.DMA
    every = range(STREAMS)
    per_token = held((s.blocks, s.steps, SUB, LANE), F32)
    expanded = (s.steps, entries, SUB, LANE)
    edge = held((s.blocks, entries, SUB, LANE), F32)
    whole_state = held((s.blocks, s.steps, entries, SUB, LANE), F32)
    tile = (s.blocks, tokens, LANE)
    packet = held((devices, 1, (s.rows + 1) * LANE), F32)
    linked = held((devices, 1, s.rows * LANE), F32)
    sums = held((2, SUB, LANE), F32)

    def exchange(send):
        return lax.all_to_all(send, "seq", 0, 0)

    def kernel(body, *more):
        return functools.partial(body, s, *more)

    offsets = [s.blocks * g for g in every]
    firsts = [
        call(
            kernel(first_kernel, offsets[g]),
            f"first_{g}",
            [
                whole_state, whole_state, held(expanded, F32),
                held((s.blocks, SUB, LANE), F32), edge, packet,
                held(tile, F32), held(tile, F32), held((entries, columns), F32),
                held((1, columns), F32), held((1, columns), F32), linked,
            ],
            [
                pltpu.VMEM(tile, F32), pltpu.VMEM(expanded, F32),
                pltpu.VMEM((2, entries, tokens), F32),
                pltpu.VMEM((2, tokens, entries), F32),
                dma((s.blocks,)), dma((s.blocks,)), dma((s.blocks,)), dma((5,)),
            ],
            [
                in_hbm(x)
                for x in (
                    rhs, delta, curvature, rate, skip[None], damping[None],
                    b_proj.T, c_proj.T,
                )
            ],
            2,
            n_hbm=8,
        )
        for g in every
    ]
    decay, drive, cx, total, e, send, rhs_v, curv, rates, skips, damps, link_rate = zip(
        *firsts
    )

    def link(g, got, backward, letter, decays=None):
        first = decays is None
        return call(
            kernel(link_kernel, backward, first),
            f"link_{letter}_{g}",
            [linked, linked if first else sums],
            [],
            (got, link_rate[g] if first else decays),
            1,
        )

    def around(send, backward, letter, decays):
        got = [exchange(send[g]) for g in every]
        pairs = [link(g, got[g], backward, letter, decays and decays[g]) for g in every]
        return [exchange(pairs[g][0]) for g in every], [pairs[g][1] for g in every]

    def common(g, e, arrive):
        return (decay[g], drive[g], cx[g], total[g], e[g], arrive[g])

    def consts(g):
        return (rates[g], skips[g], damps[g])

    arrive, decays = around(send, False, "a", None)
    e, send, w, y0 = zip(
        *[
            call(
                kernel(forward_kernel, offsets[g], True),
                f"forward_a_{g}",
                [edge, packet, per_token, per_token],
                [],
                (rhs_v[g], curv[g], *consts(g), *common(g, e, arrive)),
                2,
            )
            for g in every
        ]
    )
    arrive, sums_b = around(send, True, "b", decays)
    e, send, r = zip(
        *[
            call(
                kernel(backward_kernel, offsets[g]),
                f"backward_a_{g}",
                [edge, packet, per_token],
                [],
                (rhs_v[g], *consts(g), *common(g, e, arrive), w[g], *sums_b),
                2,
            )
            for g in every
        ]
    )
    arrive, sums_c = around(send, False, "c", decays)
    e, send, w, d = zip(
        *[
            call(
                kernel(forward_kernel, offsets[g], False),
                f"forward_b_{g}",
                [edge, packet, per_token, per_token],
                [],
                (
                    rhs_v[g], curv[g], *consts(g), *common(g, e, arrive),
                    r[g], y0[g], *sums_b, *sums_c,
                ),
                2,
            )
            for g in every
        ]
    )
    arrive, sums_d = around(send, True, "d", decays)
    outs = ()
    for g in every:
        args = (
            rhs_v[g], *consts(g), *common(g, e, arrive), w[g], r[g], d[g],
            *sums_b, *sums_c, *sums_d,
        )
        outs = pl.pallas_call(
            kernel(last_kernel, offsets[g]),
            name=f"backward_b_{g}",
            out_shape=[jax.ShapeDtypeStruct((tokens, columns), F32)] * 2,
            in_specs=[VM] * len(args) + [HBM] * len(outs),
            out_specs=[HBM] * 2,
            scratch_shapes=[
                pltpu.VMEM(tile, F32), pltpu.VMEM(tile, F32),
                dma((s.blocks,)), dma((s.blocks,)),
            ],
            input_output_aliases={len(args): 0, len(args) + 1: 1} if outs else {},
            compiler_params=pltpu.CompilerParams(vmem_limit_bytes=LIMIT),
        )(*args, *outs)
    return tuple(outs)


def solution(mesh):
    placed = (
        P("seq", None),
        P(),
        P("seq", None),
        P("seq", None),
        P("seq", None),
        P(),
        P("seq", None),
        P(),
    )
    return jax.shard_map(
        functools.partial(per_device, mesh.shape["seq"]),
        mesh=mesh,
        in_specs=placed,
        out_specs=(P("seq", None), P("seq", None)),
        check_vma=False,
    )
```

```python
import functools

import jax
import jax.numpy as jnp
from jax import lax
from jax.experimental import pallas as pl
from jax.experimental.pallas import tpu as pltpu
from jax.sharding import PartitionSpec as P

STREAMS = 1
SUB, LANE = 8, 128
LOG2E = 1.4426950408889634
HALF = -0.5 * 0.6931471805599453
F32 = jnp.float32


def sub_index():
    return lax.broadcasted_iota(jnp.int32, (SUB, LANE), 0)


def spread(row):
    return jnp.broadcast_to(row, (SUB, LANE))


def rolled(x, shift):
    return pltpu.roll(x, shift % SUB, 0)


def scan_chunks(value, decay, backward):
    at = sub_index()
    edge = at == (SUB - 1 if backward else 0)
    keep = jnp.where(edge, 0.0, decay)
    for step in (1, 2, 4):
        shift = -step if backward else step
        value = value + keep * rolled(value, shift)
        if step < 4:
            keep = keep * rolled(keep, shift)
    entering = jnp.where(edge, 0.0, rolled(value, -1 if backward else 1))
    last = value[0:1] if backward else value[SUB - 1 : SUB]
    return entering, last


def total_around(total, backward):
    at = sub_index()
    edge = at == (SUB - 1 if backward else 0)
    side = -1 if backward else 1
    value = jnp.where(edge, 0.0, rolled(total, side))
    for step in (1, 2, 4):
        inside = at < SUB - step if backward else at >= step
        value = value + jnp.where(inside, rolled(value, side * step), 0.0)
    return value


def summed(parts):
    while len(parts) > 1:
        parts = [sum(parts[i : i + 2]) for i in range(0, len(parts), 2)]
    return parts[0]


class Sizes:
    def __init__(self, tokens, columns, entries, devices, streams):
        self.tokens, self.entries, self.devices = tokens, entries, devices
        self.steps = tokens // SUB
        self.blocks = columns // LANE // streams
        self.half = self.blocks // 2
        self.levels = []
        stride = 2
        while stride < devices:
            radix = 4 if devices // stride % 4 == 0 else 2
            self.levels.append((stride, radix))
            stride *= radix


def cols(block):
    return pl.ds(pl.multiple_of(block * LANE, LANE), LANE)


def my_core():
    return lax.axis_index("seq") & 1


def place_of(s, block):
    upper = (block >= s.half).astype(jnp.int32)
    return upper ^ my_core(), block - upper * s.half


def write_state(s, both_ref, block, rows_of):
    slot, place = place_of(s, block)
    for n, value in enumerate(rows_of):
        both_ref[slot, place, n : n + 1, :] = value


def over_blocks(s, scans, body, carry):
    for upper, scan in enumerate(scans):

        def one(place, carry, upper=upper, scan=scan):
            return body(upper * s.half + place, scan, place, carry)

        carry = lax.fori_loop(0, s.half, one, carry)
    return carry


def part_packets(both_ref, keep_ref, give_ref):
    keep_ref[...] = both_ref[0]
    give_ref[...] = both_ref[1]


def gather_state(s, arrive, arrive_ref):
    own_ref, got_ref = arrive
    for slot, ref in ((my_core(), own_ref), (1 - my_core(), got_ref)):
        arrive_ref[pl.ds(slot * s.half, s.half)] = ref[...]


def read_state(s, arrive_ref, block):
    return [spread(arrive_ref[block, n : n + 1, :]) for n in range(s.entries)]


def load_rates(s, rate_ref, block):
    return [spread(rate_ref[n : n + 1, cols(block)]) for n in range(s.entries)]


def finish_summary(s, block, state, rates, total, e_ref, put, backward):
    lasts = []
    for n in range(s.entries):
        entering, last = scan_chunks(state[n], jnp.exp2(total * rates[n]), backward)
        e_ref[block, n] = entering
        lasts.append(last)
    write_state(s, put, block, lasts)


def zeros(count):
    return [jnp.zeros((SUB, LANE), F32)] * count


def first_kernel(s, offset, *refs):
    rhs_hbm, delta_hbm, curv_hbm, rate_hbm, skip_hbm, damp_hbm, bt_hbm, ct_hbm = refs[:8]
    (
        low_scan, high_scan, cx_ref, total_ref, e_ref, keep_ref, give_ref,
        rhs_ref, curv_ref, rate_ref, skip_ref, damp_ref,
    ) = refs[8:20]
    delta_ref, bx_ref, wide_ref, turn_ref, sem_d, sem_v, sem_c, sem_s, put = refs[20:]
    for slot in (0, 1):
        put[slot, s.half] = jnp.zeros((s.entries, LANE), F32)

    small = [
        pltpu.make_async_copy(src, dst, sem_s.at[i])
        for i, (src, dst) in enumerate(
            [
                (bt_hbm, wide_ref.at[0]), (ct_hbm, wide_ref.at[1]), (rate_hbm, rate_ref),
                (skip_hbm, skip_ref), (damp_hbm, damp_ref),
            ]
        )
    ]

    def block_copy(src, dst, sem, block):
        return pltpu.make_async_copy(
            src.at[:, cols(block + offset)], dst.at[block], sem.at[block]
        )

    for copy in small[:3]:
        copy.start()
    for block in range(s.blocks):
        block_copy(delta_hbm, delta_ref, sem_d, block).start()
        block_copy(rhs_hbm, rhs_ref, sem_v, block).start()
    for copy in small[3:]:
        copy.start()
    for block in range(s.blocks):
        block_copy(curv_hbm, curv_ref, sem_c, block).start()

    for index, dst in enumerate([bx_ref, cx_ref]):
        small[index].wait()
        turn_ref[index] = jnp.transpose(wide_ref[index])
        for j in range(s.steps):
            turned = turn_ref[index, pl.ds(j, SUB, stride=s.steps), :]
            for n in range(s.entries):
                dst[j, n] = jnp.broadcast_to(turned[:, n : n + 1], (SUB, LANE))
    small[2].wait()
    rate_ref[...] = rate_ref[...] * (-LOG2E)

    def body(block, scan, place, carry):
        block_copy(delta_hbm, delta_ref, sem_d, block).wait()
        block_copy(rhs_hbm, rhs_ref, sem_v, block).wait()
        own = [rate_ref[n : n + 1, cols(block + offset)] for n in range(s.entries)]
        rates = [spread(row) for row in own]

        def advance(j, state):
            total, state = state[0], list(state[1:])
            rows = pl.ds(j, SUB, stride=s.steps)
            d = delta_ref[block, rows, :]
            v = rhs_ref[block, rows, :]
            total = total + d
            for n in range(s.entries):
                z = d * rates[n]
                decay = jnp.exp2(z)
                drive = jnp.tanh(z * HALF) * (bx_ref[j, n] * (1.0 + decay))
                scan[place, j, n, 0] = decay
                scan[place, j, n, 1] = drive
                state[n] = decay * state[n] + drive * v
            return (total, *state)

        result = lax.fori_loop(0, s.steps, advance, tuple(zeros(s.entries + 1)), unroll=16)
        total, state = result[0], result[1:]
        total_ref[block] = total
        finish_summary(s, block, state, rates, total, e_ref, put, False)
        whole = jnp.sum(total, axis=0, keepdims=True)
        slot, row = place_of(s, block)
        put[slot, s.half, pl.ds(row, 1), :] = whole
        return carry

    over_blocks(s, (low_scan, high_scan), body, 0)
    part_packets(put, keep_ref, give_ref)
    small[3].wait()
    small[4].wait()

    def finish(block, carry):
        block_copy(curv_hbm, curv_ref, sem_c, block).wait()
        return carry

    lax.fori_loop(0, s.blocks, finish, 0)


def put_sums(s, put, keep_ref, give_ref, first, second):
    first = jnp.sum(first, axis=0, keepdims=True)
    second = jnp.sum(second, axis=0, keepdims=True)
    for slot in (0, 1):
        put[slot, s.half] = jnp.zeros((s.entries, LANE), F32)
        put[slot, s.half, 0:1, :] = first
        put[slot, s.half, 1:2, :] = second
    part_packets(put, keep_ref, give_ref)


def half_rates(s, rate_ref, block):
    return rate_ref[:, cols(my_core() * s.half + block)]


def join_kernel(s, backward, first, *refs):
    if first:
        keep_ref, got_ref, rate_ref, chip_ref, core_ref = refs
    else:
        keep_ref, got_ref, core_ref, chip_ref = refs
    low = my_core() == 0
    for block in range(s.half):
        keep, got = keep_ref[block], got_ref[block]
        if first:
            rates = half_rates(s, rate_ref, block)
            mine = keep_ref[s.half, block : block + 1, :]
            other = got_ref[s.half, block : block + 1, :]
            core_ref[0, block] = jnp.exp2(rates * jnp.where(low, mine, other))
            core_ref[1, block] = jnp.exp2(rates * jnp.where(low, other, mine))
        near = jnp.where(low, got, keep) if backward else jnp.where(low, keep, got)
        far = jnp.where(low, keep, got) if backward else jnp.where(low, got, keep)
        chip_ref[block] = core_ref[0 if backward else 1, block] * near + far
    chip_ref[s.half] = keep_ref[s.half] + got_ref[s.half]


def level_weights(s, stride, radix, packets, rate_ref, around_in, weight_ref, around_ref):
    digit = lax.rem(lax.axis_index("seq") // stride, radix)
    digits = [digit ^ k for k in range(radix)]
    times = [packet[s.half, 0 : s.half, :] for packet in packets]
    none = jnp.zeros_like(times[0])

    def gathered(test):
        return sum(jnp.where(test(d), t, 0.0) for d, t in zip(digits, times))

    rates = [half_rates(s, rate_ref, block) for block in range(s.half)]
    for side in (0, 1):
        def beyond(a, b):
            return a < b if side else a > b

        start = around_in[side] if around_in is not None else none
        for k in range(radix):
            span = gathered(lambda d: beyond(d, digits[k]))
            for block in range(s.half):
                weight_ref[side, radix - 1 + k, block] = jnp.exp2(
                    rates[block] * span[block : block + 1]
                )
            if k:
                on = beyond(digit, digits[k])
                gap = start + gathered(
                    lambda d: jnp.logical_and(beyond(d, digits[k]), beyond(digit, d))
                )
                for block in range(s.half):
                    weight_ref[side, k - 1, block] = jnp.where(
                        on, jnp.exp2(rates[block] * gap[block : block + 1]), 0.0
                    )
        around_ref[side] = start + gathered(lambda d: beyond(digit, d))


def level_kernel(s, level, backward, first, *refs):
    stride, radix = s.levels[level]
    last = level == len(s.levels) - 1
    refs = list(refs)
    packets, refs = refs[:radix], refs[radix:]
    arrive_in = around_in = None
    if level:
        arrive_in = refs.pop(0)
    if first:
        rate_ref = refs.pop(0)
        if level:
            around_in = refs.pop(0)
    else:
        weight_ref = refs.pop(0)
    if last:
        keep_ref, got_ref, core_ref = refs[:3]
        own_ref, give_ref, sums_ref = refs[3:6]
        refs = refs[6:]
    else:
        group_ref, arrive_ref = refs[:2]
        refs = refs[2:]
    if first:
        weight_ref, around_ref = refs
        level_weights(
            s, stride, radix, packets, rate_ref, around_in, weight_ref, around_ref
        )
    side = 1 if backward else 0
    low = my_core() == 0
    for block in range(s.half):
        values = [packet[block] for packet in packets]
        arrive = summed(
            [weight_ref[side, k - 1, block] * values[k] for k in range(1, radix)]
        )
        if level:
            arrive = arrive_in[block] + arrive
        if not last:
            arrive_ref[block] = arrive
            group_ref[block] = summed(
                [weight_ref[side, radix - 1 + k, block] * values[k] for k in range(radix)]
            )
            continue
        keep, got = keep_ref[block], got_ref[block]
        near = jnp.where(low, got, keep) if backward else jnp.where(low, keep, got)
        far = core_ref[side, block] * arrive + near
        at_near = jnp.logical_not(low) if backward else low
        own_ref[block] = jnp.where(at_near, arrive, far)
        give_ref[block] = jnp.where(at_near, far, arrive)
    spare = summed([packet[s.half] for packet in packets])
    if last:
        whole = jnp.sum(spare[0:SUB], axis=1, keepdims=True)
        sums_ref[0] = jnp.broadcast_to(whole[0:1], (SUB, LANE))
        sums_ref[1] = jnp.broadcast_to(whole[1:2], (SUB, LANE))
    else:
        group_ref[s.half] = spare


def total_sum(sums, index):
    return sum(ref[index] for ref in sums)


def enter(s, arrive_ref, e_ref, block, rates, around):
    arrive = read_state(s, arrive_ref, block)
    return [
        e_ref[block, n] + jnp.exp2(around * rates[n]) * arrive[n]
        for n in range(s.entries)
    ]


def forward_kernel(s, offset, first, *refs):
    refs = list(refs)
    rhs_ref, curv_ref, rate_ref, skip_ref, damp_ref = refs[:5]
    low_scan, high_scan, cx_ref, total_ref, e_in = refs[5:10]
    arrive, refs = refs[10:12], refs[12:]
    if not first:
        r_ref, y0_ref = refs[:2]
        sums_b, sums_c = refs[2 : 2 + STREAMS], refs[2 + STREAMS : 2 + 2 * STREAMS]
        refs = refs[2 + 2 * STREAMS :]
        ratio = total_sum(sums_c, 0) / total_sum(sums_b, 0)
    e_out, keep_ref, give_ref, w_ref, y_ref, put, arrive_ref = refs
    gather_state(s, arrive, arrive_ref)

    def body(block, scan, place, carry):
        squares, inner = carry
        rates = load_rates(s, rate_ref, block + offset)
        total = total_ref[block]
        skip = spread(skip_ref[0:1, cols(block + offset)])
        damp = spread(damp_ref[0:1, cols(block + offset)])
        before = total_around(total, False)
        state = enter(s, arrive_ref, e_in, block, rates, before)
        for j in range(s.steps):
            rows = pl.ds(j, SUB, stride=s.steps)
            rhs = rhs_ref[block, rows, :]
            v = rhs if first else r_ref[block, j]
            parts = [skip * v]
            for n in range(s.entries):
                state[n] = (
                    scan[place, j, n, 0] * state[n] + scan[place, j, n, 1] * v
                )
                parts.append(cx_ref[j, n] * state[n])
            y = summed(parts)
            if first:
                y_ref[block, j] = y
                squares = squares + v * v
                along = v
            else:
                y = y + ratio * y0_ref[block, j]
                along = v + ratio * rhs
                y_ref[block, j] = along
            w = curv_ref[block, rows, :] * y
            w_ref[block, j] = w
            inner = inner + (w * y + damp * (along * along))

        passed = zeros(s.entries)
        for j in reversed(range(s.steps)):
            w = w_ref[block, j]
            for n in range(s.entries):
                passed[n] = scan[place, j, n, 0] * (cx_ref[j, n] * w + passed[n])
        finish_summary(s, block, passed, rates, total, e_out, put, True)
        return squares, inner

    squares, inner = over_blocks(s, (low_scan, high_scan), body, tuple(zeros(2)))
    put_sums(s, put, keep_ref, give_ref, squares, inner)


def backward_block(s, block, scan, place, w_ref, skip, cx_ref, passed, use):
    for j in reversed(range(s.steps)):
        w = w_ref[block, j]
        parts = [skip * w]
        for n in range(s.entries):
            costate = cx_ref[j, n] * w + passed[n]
            passed[n] = scan[place, j, n, 0] * costate
            parts.append(scan[place, j, n, 1] * costate)
        use(j, summed(parts))


def backward_kernel(s, offset, *refs):
    rhs_ref, rate_ref, skip_ref, damp_ref = refs[:4]
    low_scan, high_scan, cx_ref, total_ref, e_in = refs[4:9]
    arrive, w_ref = refs[9:11], refs[11]
    sums_b = refs[12 : 12 + STREAMS]
    e_out, keep_ref, give_ref, r_ref, put, arrive_ref = refs[12 + STREAMS :]
    gather_state(s, arrive, arrive_ref)
    step = total_sum(sums_b, 0) / total_sum(sums_b, 1)

    def body(block, scan, place, squares):
        rates = load_rates(s, rate_ref, block + offset)
        total = total_ref[block]
        skip = spread(skip_ref[0:1, cols(block + offset)])
        damp = spread(damp_ref[0:1, cols(block + offset)])
        after = total_around(total, True)
        passed = enter(s, arrive_ref, e_in, block, rates, after)
        acc = [squares]

        def use(j, product):
            v = rhs_ref[block, pl.ds(j, SUB, stride=s.steps), :]
            r = v - step * (product + damp * v)
            r_ref[block, j] = r
            acc[0] = acc[0] + r * r

        backward_block(s, block, scan, place, w_ref, skip, cx_ref, passed, use)
        state = zeros(s.entries)
        for j in range(s.steps):
            v = r_ref[block, j]
            for n in range(s.entries):
                state[n] = (
                    scan[place, j, n, 0] * state[n] + scan[place, j, n, 1] * v
                )
        finish_summary(s, block, state, rates, total, e_out, put, False)
        return acc[0]

    squares = over_blocks(s, (low_scan, high_scan), body, zeros(1)[0])
    put_sums(s, put, keep_ref, give_ref, squares, zeros(1)[0])


def last_kernel(s, offset, *refs):
    rhs_ref, rate_ref, skip_ref, damp_ref = refs[:4]
    low_scan, high_scan, cx_ref, total_ref, e_in = refs[4:9]
    arrive, w_ref = refs[9:11], refs[11]
    r_ref, d_ref = refs[12:14]
    refs = refs[14:]
    sums_b, sums_c = refs[:STREAMS], refs[STREAMS : 2 * STREAMS]
    sums_d = refs[2 * STREAMS : 3 * STREAMS]
    refs = refs[3 * STREAMS :]
    if offset:
        refs = refs[2:]
    solution_ref, residual_ref, tile_s, tile_r, sem_s, sem_r, arrive_ref = refs
    gather_state(s, arrive, arrive_ref)
    before_step = total_sum(sums_b, 0) / total_sum(sums_b, 1)
    step = total_sum(sums_c, 0) / total_sum(sums_d, 1)

    def copies(block):
        where = cols(block + offset)
        return (
            pltpu.make_async_copy(
                tile_s.at[block], solution_ref.at[:, where], sem_s.at[block]
            ),
            pltpu.make_async_copy(
                tile_r.at[block], residual_ref.at[:, where], sem_r.at[block]
            ),
        )

    def body(block, scan, place, carry):
        rates = load_rates(s, rate_ref, block + offset)
        skip = spread(skip_ref[0:1, cols(block + offset)])
        damp = spread(damp_ref[0:1, cols(block + offset)])
        after = total_around(total_ref[block], True)
        passed = enter(s, arrive_ref, e_in, block, rates, after)

        def use(j, product):
            rows = pl.ds(j, SUB, stride=s.steps)
            along = d_ref[block, j]
            tile_s[block, rows, :] = (
                before_step * rhs_ref[block, rows, :] + step * along
            )
            tile_r[block, rows, :] = r_ref[block, j] - step * (product + damp * along)

        backward_block(s, block, scan, place, w_ref, skip, cx_ref, passed, use)
        for copy in copies(block):
            copy.start()
        return carry

    over_blocks(s, (low_scan, high_scan), body, 0)

    def finish(block, carry):
        for copy in copies(block):
            copy.wait()
        return carry

    lax.fori_loop(0, s.blocks, finish, 0)


VM = pl.BlockSpec(memory_space=pltpu.VMEM)
HBM = pl.BlockSpec(memory_space=pltpu.HBM)
LIMIT = 6 * 1024 * 1024


def in_hbm(x):
    return pltpu.with_memory_space_constraint(x, pltpu.HBM)


def call(body, name, outs, scratch, args, passes, n_hbm=0, out_specs=None, aliases=()):
    work = int(passes * 16 * 128 * 2048)
    return pl.pallas_call(
        body,
        name=name,
        out_shape=outs,
        in_specs=[HBM] * n_hbm + [VM] * (len(args) - n_hbm),
        out_specs=out_specs or [VM] * len(outs),
        scratch_shapes=scratch,
        input_output_aliases=dict(aliases),
        cost_estimate=pl.CostEstimate(
            flops=work, bytes_accessed=work, transcendentals=0
        ),
        compiler_params=pltpu.CompilerParams(vmem_limit_bytes=LIMIT),
    )(*args)


def per_device(devices, rhs, rate, delta, b_proj, c_proj, skip, curvature, damping):
    tokens, columns = rhs.shape
    entries = rate.shape[0]
    s = Sizes(tokens, columns, entries, devices, STREAMS)
    held = pltpu.VMEM
    dma = pltpu.SemaphoreType.DMA
    every = range(STREAMS)
    per_token = held((s.blocks, s.steps, SUB, LANE), F32)
    expanded = (s.steps, entries, SUB, LANE)
    edge = held((s.blocks, entries, SUB, LANE), F32)
    half_state = held((s.half, s.steps, entries, 2, SUB, LANE), F32)
    tile = (s.blocks, tokens, LANE)
    packet = held((s.half + 1, entries, LANE), F32)
    linked = held((s.half, entries, LANE), F32)
    sums = held((2, SUB, LANE), F32)
    both = pltpu.VMEM((2, s.half + 1, entries, LANE), F32)
    joined = pltpu.VMEM((s.blocks, entries, LANE), F32)

    def swap(send, distance):
        pairs = [(device, device ^ distance) for device in range(devices)]
        return lax.ppermute(send, "seq", pairs)

    def kernel(body, *more):
        return functools.partial(body, s, *more)

    offsets = [s.blocks * g for g in every]
    firsts = [
        call(
            kernel(first_kernel, offsets[g]),
            f"first_{g}",
            [
                half_state, half_state, held(expanded, F32),
                held((s.blocks, SUB, LANE), F32), edge, packet, packet,
                held(tile, F32), held(tile, F32), held((entries, columns), F32),
                held((1, columns), F32), held((1, columns), F32),
            ],
            [
                pltpu.VMEM(tile, F32), pltpu.VMEM(expanded, F32),
                pltpu.VMEM((2, entries, tokens), F32),
                pltpu.VMEM((2, tokens, entries), F32),
                dma((s.blocks,)), dma((s.blocks,)), dma((s.blocks,)), dma((5,)),
                both,
            ],
            [
                in_hbm(x)
                for x in (
                    rhs, delta, curvature, rate, skip[None], damping[None],
                    b_proj.T, c_proj.T,
                )
            ],
            2,
            n_hbm=8,
        )
        for g in every
    ]
    (
        low_scan, high_scan, cx, total, e, keep, give, rhs_v, curv, rates, skips, damps,
    ) = zip(*firsts)

    def around(keep, give, backward, letter, known):
        (keep,), (give,) = keep, give
        first = known is None
        made = []
        got = swap(give, 1)
        outs = [packet] + [held((2, s.half, entries, LANE), F32)] * first
        chip = call(
            kernel(join_kernel, backward, first),
            f"join_{letter}",
            outs,
            [],
            (keep, got, rates[0] if first else known[0]),
            0.02,
        )
        core = chip[1] if first else known[0]
        group, arrive, passing = chip[0], None, None
        for level, (stride, radix) in enumerate(s.levels):
            last = level == len(s.levels) - 1
            packets = [group] + [swap(group, stride * k) for k in range(1, radix)]
            args = packets + [arrive] * (level > 0)
            args += [rates[0] if first else known[1 + level]]
            args += [passing] * (first and level > 0)
            outs = [linked, linked, sums] if last else [packet, linked]
            if last:
                args += [keep, got, core]
            if first:
                outs = outs + [
                    held((2, 2 * radix - 1, s.half, entries, LANE), F32),
                    held((2, s.half, LANE), F32),
                ]
            results = call(
                kernel(level_kernel, level, backward, first),
                f"level_{level}_{letter}",
                outs,
                [],
                args,
                0.02,
            )
            if first:
                *results, weights, passing = results
                made.append(weights)
            group, arrive = results[:2]
        own, give_back, total = results
        return (own, swap(give_back, 1)), [total], known or [core, *made]

    def common(g, e, arrive):
        return (low_scan[g], high_scan[g], cx[g], total[g], e[g], *arrive)

    def consts(g):
        return (rates[g], skips[g], damps[g])

    arrive, _, known = around(keep, give, False, "a", None)
    e, keep, give, w, y0 = zip(
        *[
            call(
                kernel(forward_kernel, offsets[g], True),
                f"forward_a_{g}",
                [edge, packet, packet, per_token, per_token],
                [both, joined],
                (rhs_v[g], curv[g], *consts(g), *common(g, e, arrive)),
                2,
            )
            for g in every
        ]
    )
    arrive, sums_b, _ = around(keep, give, True, "b", known)
    e, keep, give, r = zip(
        *[
            call(
                kernel(backward_kernel, offsets[g]),
                f"backward_a_{g}",
                [edge, packet, packet, per_token],
                [both, joined],
                (rhs_v[g], *consts(g), *common(g, e, arrive), w[g], *sums_b),
                2,
            )
            for g in every
        ]
    )
    arrive, sums_c, _ = around(keep, give, False, "c", known)
    e, keep, give, w, d = zip(
        *[
            call(
                kernel(forward_kernel, offsets[g], False),
                f"forward_b_{g}",
                [edge, packet, packet, per_token, per_token],
                [both, joined],
                (
                    rhs_v[g], curv[g], *consts(g), *common(g, e, arrive),
                    r[g], y0[g], *sums_b, *sums_c,
                ),
                2,
            )
            for g in every
        ]
    )
    arrive, sums_d, _ = around(keep, give, True, "d", known)
    outs = ()
    for g in every:
        args = (
            rhs_v[g], *consts(g), *common(g, e, arrive), w[g], r[g], d[g],
            *sums_b, *sums_c, *sums_d,
        )
        outs = pl.pallas_call(
            kernel(last_kernel, offsets[g]),
            name=f"backward_b_{g}",
            out_shape=[jax.ShapeDtypeStruct((tokens, columns), F32)] * 2,
            in_specs=[VM] * len(args) + [HBM] * len(outs),
            out_specs=[HBM] * 2,
            scratch_shapes=[
                pltpu.VMEM(tile, F32), pltpu.VMEM(tile, F32),
                dma((s.blocks,)), dma((s.blocks,)), joined,
            ],
            input_output_aliases={len(args): 0, len(args) + 1: 1} if outs else {},
            compiler_params=pltpu.CompilerParams(vmem_limit_bytes=LIMIT),
        )(*args, *outs)
    return tuple(outs)


def solution(mesh):
    placed = (
        P("seq", None),
        P(),
        P("seq", None),
        P("seq", None),
        P("seq", None),
        P(),
        P("seq", None),
        P(),
    )
    return jax.shard_map(
        functools.partial(per_device, mesh.shape["seq"]),
        mesh=mesh,
        in_specs=placed,
        out_specs=(P("seq", None), P("seq", None)),
        check_vma=False,
    )
```

```python
import functools

import jax
import jax.numpy as jnp
from jax import lax
from jax.experimental import pallas as pl
from jax.experimental.pallas import tpu as pltpu
from jax.sharding import PartitionSpec as P

STREAMS = 1
SUB, LANE = 8, 128
LOG2E = 1.4426950408889634
HALF = -0.5 * 0.6931471805599453
F32 = jnp.float32


def sub_index():
    return lax.broadcasted_iota(jnp.int32, (SUB, LANE), 0)


def spread(row):
    return jnp.broadcast_to(row, (SUB, LANE))


def rolled(x, shift):
    return pltpu.roll(x, shift % SUB, 0)


def scan_chunks(value, decay, backward):
    at = sub_index()
    edge = at == (SUB - 1 if backward else 0)
    keep = jnp.where(edge, 0.0, decay)
    for step in (1, 2, 4):
        shift = -step if backward else step
        value = value + keep * rolled(value, shift)
        if step < 4:
            keep = keep * rolled(keep, shift)
    entering = jnp.where(edge, 0.0, rolled(value, -1 if backward else 1))
    last = value[0:1] if backward else value[SUB - 1 : SUB]
    return entering, last


def total_around(total, backward):
    at = sub_index()
    edge = at == (SUB - 1 if backward else 0)
    side = -1 if backward else 1
    value = jnp.where(edge, 0.0, rolled(total, side))
    for step in (1, 2, 4):
        inside = at < SUB - step if backward else at >= step
        value = value + jnp.where(inside, rolled(value, side * step), 0.0)
    return value


def summed(parts):
    while len(parts) > 1:
        parts = [sum(parts[i : i + 2]) for i in range(0, len(parts), 2)]
    return parts[0]


class Sizes:
    def __init__(self, tokens, columns, entries, devices, streams):
        self.tokens, self.entries, self.devices = tokens, entries, devices
        self.steps = tokens // SUB
        self.blocks = columns // LANE // streams
        self.half = self.blocks // 2
        self.levels = []
        stride = 2
        while stride < devices:
            radix = 4 if devices // stride % 4 == 0 else 2
            self.levels.append((stride, radix))
            stride *= radix


def cols(block):
    return pl.ds(pl.multiple_of(block * LANE, LANE), LANE)


def my_core():
    return lax.axis_index("seq") & 1


def place_of(s, block):
    upper = (block >= s.half).astype(jnp.int32)
    return upper ^ my_core(), block - upper * s.half


def write_state(s, both_ref, block, rows_of):
    slot, place = place_of(s, block)
    if not isinstance(both_ref, tuple):
        for n, value in enumerate(rows_of):
            both_ref[slot, place, n : n + 1, :] = value
        return
    for index, ref in enumerate(both_ref):

        @pl.when(slot == index)
        def _(ref=ref):
            for n, value in enumerate(rows_of):
                ref[place, n : n + 1, :] = value


def over_blocks(s, scans, body, carry):
    for upper, scan in enumerate(scans):

        def one(place, carry, upper=upper, scan=scan):
            return body(upper * s.half + place, scan, place, carry)

        carry = lax.fori_loop(0, s.half, one, carry)
    return carry


def part_packets(both_ref, keep_ref, give_ref):
    keep_ref[...] = both_ref[0]
    give_ref[...] = both_ref[1]


def gather_state(s, arrive, arrive_ref):
    own_ref, got_ref = arrive
    for slot, ref in ((my_core(), own_ref), (1 - my_core(), got_ref)):
        arrive_ref[pl.ds(slot * s.half, s.half)] = ref[...]


def read_state(s, arrive_ref, block):
    return [spread(arrive_ref[block, n : n + 1, :]) for n in range(s.entries)]


def load_rates(s, rate_ref, block):
    return [spread(rate_ref[n : n + 1, cols(block)]) for n in range(s.entries)]


def finish_summary(s, block, state, rates, total, e_ref, put, backward):
    lasts = []
    for n in range(s.entries):
        entering, last = scan_chunks(state[n], jnp.exp2(total * rates[n]), backward)
        e_ref[block, n] = entering
        lasts.append(last)
    write_state(s, put, block, lasts)


def zeros(count):
    return [jnp.zeros((SUB, LANE), F32)] * count


def first_kernel(s, offset, *refs):
    rhs_hbm, delta_hbm, curv_hbm, rate_hbm, skip_hbm, damp_hbm, bt_hbm, ct_hbm = refs[:8]
    (
        low_scan, high_scan, cx_ref, total_ref, e_ref, keep_ref, give_ref,
        rhs_ref, curv_ref, rate_ref, skip_ref, damp_ref,
    ) = refs[8:20]
    delta_ref, bx_ref, wide_ref, turn_ref, sem_d, sem_v, sem_c, sem_s = refs[20:]
    put = keep_ref, give_ref
    for ref in put:
        ref[s.half] = jnp.zeros((s.entries, LANE), F32)

    small = [
        pltpu.make_async_copy(src, dst, sem_s.at[i])
        for i, (src, dst) in enumerate(
            [
                (bt_hbm, wide_ref.at[0]), (ct_hbm, wide_ref.at[1]), (rate_hbm, rate_ref),
                (skip_hbm, skip_ref), (damp_hbm, damp_ref),
            ]
        )
    ]

    def block_copy(src, dst, sem, block):
        return pltpu.make_async_copy(
            src.at[:, cols(block + offset)], dst.at[block], sem.at[block]
        )

    for copy in small[:3]:
        copy.start()
    for block in range(s.blocks):
        block_copy(delta_hbm, delta_ref, sem_d, block).start()
        block_copy(rhs_hbm, rhs_ref, sem_v, block).start()
    for copy in small[3:]:
        copy.start()
    for block in range(s.blocks):
        block_copy(curv_hbm, curv_ref, sem_c, block).start()

    for index, dst in enumerate([bx_ref, cx_ref]):
        small[index].wait()
        turn_ref[index] = jnp.transpose(wide_ref[index])
        for j in range(s.steps):
            turned = turn_ref[index, pl.ds(j, SUB, stride=s.steps), :]
            for n in range(s.entries):
                dst[j, n] = jnp.broadcast_to(turned[:, n : n + 1], (SUB, LANE))
    small[2].wait()
    rate_ref[...] = rate_ref[...] * (-LOG2E)

    def body(block, scan, place, carry):
        block_copy(delta_hbm, delta_ref, sem_d, block).wait()
        block_copy(rhs_hbm, rhs_ref, sem_v, block).wait()
        own = [rate_ref[n : n + 1, cols(block + offset)] for n in range(s.entries)]
        rates = [spread(row) for row in own]

        def advance(j, state):
            total, state = state[0], list(state[1:])
            rows = pl.ds(j, SUB, stride=s.steps)
            d = delta_ref[block, rows, :]
            v = rhs_ref[block, rows, :]
            total = total + d
            for n in range(s.entries):
                z = d * rates[n]
                decay = jnp.exp2(z)
                drive = jnp.tanh(z * HALF) * (bx_ref[j, n] * (1.0 + decay))
                scan[place, j, n, 0] = decay
                scan[place, j, n, 1] = drive
                state[n] = decay * state[n] + drive * v
            return (total, *state)

        result = lax.fori_loop(0, s.steps, advance, tuple(zeros(s.entries + 1)), unroll=16)
        total, state = result[0], result[1:]
        total_ref[block] = total
        finish_summary(s, block, state, rates, total, e_ref, put, False)
        whole = jnp.sum(total, axis=0, keepdims=True)
        slot, row = place_of(s, block)
        for index, ref in enumerate(put):

            @pl.when(slot == index)
            def _(ref=ref):
                ref[s.half, pl.ds(row, 1), :] = whole

        return carry

    over_blocks(s, (low_scan, high_scan), body, 0)
    small[3].wait()
    small[4].wait()

    def finish(block, carry):
        block_copy(curv_hbm, curv_ref, sem_c, block).wait()
        return carry

    lax.fori_loop(0, s.blocks, finish, 0)


def put_sums(s, put, keep_ref, give_ref, first, second):
    first = jnp.sum(first, axis=0, keepdims=True)
    second = jnp.sum(second, axis=0, keepdims=True)
    for slot in (0, 1):
        put[slot, s.half] = jnp.zeros((s.entries, LANE), F32)
        put[slot, s.half, 0:1, :] = first
        put[slot, s.half, 1:2, :] = second
    part_packets(put, keep_ref, give_ref)


def half_rates(s, rate_ref, block):
    return rate_ref[:, cols(my_core() * s.half + block)]


def join_kernel(s, backward, first, *refs):
    if first:
        keep_ref, got_ref, rate_ref, chip_ref, core_ref = refs
    else:
        keep_ref, got_ref, core_ref, chip_ref = refs
    low = my_core() == 0
    for block in range(s.half):
        keep, got = keep_ref[block], got_ref[block]
        if first:
            rates = half_rates(s, rate_ref, block)
            mine = keep_ref[s.half, block : block + 1, :]
            other = got_ref[s.half, block : block + 1, :]
            core_ref[0, block] = jnp.exp2(rates * jnp.where(low, mine, other))
            core_ref[1, block] = jnp.exp2(rates * jnp.where(low, other, mine))
        near = jnp.where(low, got, keep) if backward else jnp.where(low, keep, got)
        far = jnp.where(low, keep, got) if backward else jnp.where(low, got, keep)
        chip_ref[block] = core_ref[0 if backward else 1, block] * near + far
    chip_ref[s.half] = keep_ref[s.half] + got_ref[s.half]


def level_weights(s, stride, radix, packets, rate_ref, around_in, weight_ref, around_ref):
    digit = lax.rem(lax.axis_index("seq") // stride, radix)
    digits = [digit ^ k for k in range(radix)]
    times = [packet[s.half, 0 : s.half, :] for packet in packets]
    none = jnp.zeros_like(times[0])

    def gathered(test):
        return sum(jnp.where(test(d), t, 0.0) for d, t in zip(digits, times))

    rates = [half_rates(s, rate_ref, block) for block in range(s.half)]
    for side in (0, 1):
        def beyond(a, b):
            return a < b if side else a > b

        start = around_in[side] if around_in is not None else none
        for k in range(radix):
            span = gathered(lambda d: beyond(d, digits[k]))
            for block in range(s.half):
                weight_ref[side, radix - 1 + k, block] = jnp.exp2(
                    rates[block] * span[block : block + 1]
                )
            if k:
                on = beyond(digit, digits[k])
                gap = start + gathered(
                    lambda d: jnp.logical_and(beyond(d, digits[k]), beyond(digit, d))
                )
                for block in range(s.half):
                    weight_ref[side, k - 1, block] = jnp.where(
                        on, jnp.exp2(rates[block] * gap[block : block + 1]), 0.0
                    )
        around_ref[side] = start + gathered(lambda d: beyond(digit, d))


def level_kernel(s, level, backward, first, *refs):
    stride, radix = s.levels[level]
    last = level == len(s.levels) - 1
    refs = list(refs)
    packets, refs = refs[:radix], refs[radix:]
    arrive_in = around_in = None
    if level:
        arrive_in = refs.pop(0)
    if first:
        rate_ref = refs.pop(0)
        if level:
            around_in = refs.pop(0)
    else:
        weight_ref = refs.pop(0)
    if last:
        keep_ref, got_ref, core_ref = refs[:3]
        own_ref, give_ref, sums_ref = refs[3:6]
        refs = refs[6:]
    else:
        group_ref, arrive_ref = refs[:2]
        refs = refs[2:]
    if first:
        weight_ref, around_ref = refs
        level_weights(
            s, stride, radix, packets, rate_ref, around_in, weight_ref, around_ref
        )
    side = 1 if backward else 0
    low = my_core() == 0
    for block in range(s.half):
        values = [packet[block] for packet in packets]
        arrive = summed(
            [weight_ref[side, k - 1, block] * values[k] for k in range(1, radix)]
        )
        if level:
            arrive = arrive_in[block] + arrive
        if not last:
            arrive_ref[block] = arrive
            group_ref[block] = summed(
                [weight_ref[side, radix - 1 + k, block] * values[k] for k in range(radix)]
            )
            continue
        keep, got = keep_ref[block], got_ref[block]
        near = jnp.where(low, got, keep) if backward else jnp.where(low, keep, got)
        far = core_ref[side, block] * arrive + near
        at_near = jnp.logical_not(low) if backward else low
        own_ref[block] = jnp.where(at_near, arrive, far)
        give_ref[block] = jnp.where(at_near, far, arrive)
    spare = summed([packet[s.half] for packet in packets])
    if last:
        whole = jnp.sum(spare[0:SUB], axis=1, keepdims=True)
        sums_ref[0] = jnp.broadcast_to(whole[0:1], (SUB, LANE))
        sums_ref[1] = jnp.broadcast_to(whole[1:2], (SUB, LANE))
    else:
        group_ref[s.half] = spare


def total_sum(sums, index):
    return sum(ref[index] for ref in sums)


def enter(s, arrive_ref, e_ref, block, rates, around):
    arrive = read_state(s, arrive_ref, block)
    return [
        e_ref[block, n] + jnp.exp2(around * rates[n]) * arrive[n]
        for n in range(s.entries)
    ]


def forward_kernel(s, offset, first, *refs):
    refs = list(refs)
    rhs_ref, curv_ref, rate_ref, skip_ref, damp_ref = refs[:5]
    low_scan, high_scan, cx_ref, total_ref, e_in = refs[5:10]
    arrive, refs = refs[10:12], refs[12:]
    if not first:
        r_ref, y0_ref = refs[:2]
        sums_b, sums_c = refs[2 : 2 + STREAMS], refs[2 + STREAMS : 2 + 2 * STREAMS]
        refs = refs[2 + 2 * STREAMS :]
        ratio = total_sum(sums_c, 0) / total_sum(sums_b, 0)
    e_out, keep_ref, give_ref, w_ref, y_ref, put, arrive_ref = refs
    gather_state(s, arrive, arrive_ref)

    def body(block, scan, place, carry):
        squares, inner = carry
        rates = load_rates(s, rate_ref, block + offset)
        total = total_ref[block]
        skip = spread(skip_ref[0:1, cols(block + offset)])
        damp = spread(damp_ref[0:1, cols(block + offset)])
        before = total_around(total, False)
        state = enter(s, arrive_ref, e_in, block, rates, before)
        for j in range(s.steps):
            rows = pl.ds(j, SUB, stride=s.steps)
            rhs = rhs_ref[block, rows, :]
            v = rhs if first else r_ref[block, j]
            parts = [skip * v]
            for n in range(s.entries):
                state[n] = (
                    scan[place, j, n, 0] * state[n] + scan[place, j, n, 1] * v
                )
                parts.append(cx_ref[j, n] * state[n])
            y = summed(parts)
            if first:
                y_ref[block, j] = y
                squares = squares + v * v
                along = v
            else:
                y = y + ratio * y0_ref[block, j]
                along = v + ratio * rhs
                y_ref[block, j] = along
            w = curv_ref[block, rows, :] * y
            w_ref[block, j] = w
            inner = inner + (w * y + damp * (along * along))

        passed = zeros(s.entries)
        for j in reversed(range(s.steps)):
            w = w_ref[block, j]
            for n in range(s.entries):
                passed[n] = scan[place, j, n, 0] * (cx_ref[j, n] * w + passed[n])
        finish_summary(s, block, passed, rates, total, e_out, put, True)
        return squares, inner

    squares, inner = over_blocks(s, (low_scan, high_scan), body, tuple(zeros(2)))
    put_sums(s, put, keep_ref, give_ref, squares, inner)


def backward_block(s, block, scan, place, w_ref, skip, cx_ref, passed, use):
    for j in reversed(range(s.steps)):
        w = w_ref[block, j]
        parts = [skip * w]
        for n in range(s.entries):
            costate = cx_ref[j, n] * w + passed[n]
            passed[n] = scan[place, j, n, 0] * costate
            parts.append(scan[place, j, n, 1] * costate)
        use(j, summed(parts))


def backward_kernel(s, offset, *refs):
    rhs_ref, rate_ref, skip_ref, damp_ref = refs[:4]
    low_scan, high_scan, cx_ref, total_ref, e_in = refs[4:9]
    arrive, w_ref = refs[9:11], refs[11]
    sums_b = refs[12 : 12 + STREAMS]
    e_out, keep_ref, give_ref, r_ref, put, arrive_ref = refs[12 + STREAMS :]
    gather_state(s, arrive, arrive_ref)
    step = total_sum(sums_b, 0) / total_sum(sums_b, 1)

    def body(block, scan, place, squares):
        rates = load_rates(s, rate_ref, block + offset)
        total = total_ref[block]
        skip = spread(skip_ref[0:1, cols(block + offset)])
        damp = spread(damp_ref[0:1, cols(block + offset)])
        after = total_around(total, True)
        passed = enter(s, arrive_ref, e_in, block, rates, after)
        acc = [squares]

        def use(j, product):
            v = rhs_ref[block, pl.ds(j, SUB, stride=s.steps), :]
            r = v - step * (product + damp * v)
            r_ref[block, j] = r
            acc[0] = acc[0] + r * r

        backward_block(s, block, scan, place, w_ref, skip, cx_ref, passed, use)
        state = zeros(s.entries)
        for j in range(s.steps):
            v = r_ref[block, j]
            for n in range(s.entries):
                state[n] = (
                    scan[place, j, n, 0] * state[n] + scan[place, j, n, 1] * v
                )
        finish_summary(s, block, state, rates, total, e_out, put, False)
        return acc[0]

    squares = over_blocks(s, (low_scan, high_scan), body, zeros(1)[0])
    put_sums(s, put, keep_ref, give_ref, squares, zeros(1)[0])


def last_kernel(s, offset, *refs):
    rhs_ref, rate_ref, skip_ref, damp_ref = refs[:4]
    low_scan, high_scan, cx_ref, total_ref, e_in = refs[4:9]
    arrive, w_ref = refs[9:11], refs[11]
    r_ref, d_ref = refs[12:14]
    refs = refs[14:]
    sums_b, sums_c = refs[:STREAMS], refs[STREAMS : 2 * STREAMS]
    sums_d = refs[2 * STREAMS : 3 * STREAMS]
    refs = refs[3 * STREAMS :]
    if offset:
        refs = refs[2:]
    solution_ref, residual_ref, tile_s, tile_r, sem_s, sem_r, arrive_ref = refs
    gather_state(s, arrive, arrive_ref)
    before_step = total_sum(sums_b, 0) / total_sum(sums_b, 1)
    step = total_sum(sums_c, 0) / total_sum(sums_d, 1)

    def copies(block):
        where = cols(block + offset)
        return (
            pltpu.make_async_copy(
                tile_s.at[block], solution_ref.at[:, where], sem_s.at[block]
            ),
            pltpu.make_async_copy(
                tile_r.at[block], residual_ref.at[:, where], sem_r.at[block]
            ),
        )

    def body(block, scan, place, carry):
        rates = load_rates(s, rate_ref, block + offset)
        skip = spread(skip_ref[0:1, cols(block + offset)])
        damp = spread(damp_ref[0:1, cols(block + offset)])
        after = total_around(total_ref[block], True)
        passed = enter(s, arrive_ref, e_in, block, rates, after)

        def use(j, product):
            rows = pl.ds(j, SUB, stride=s.steps)
            along = d_ref[block, j]
            tile_s[block, rows, :] = (
                before_step * rhs_ref[block, rows, :] + step * along
            )
            tile_r[block, rows, :] = r_ref[block, j] - step * (product + damp * along)

        backward_block(s, block, scan, place, w_ref, skip, cx_ref, passed, use)
        for copy in copies(block):
            copy.start()
        return carry

    over_blocks(s, (low_scan, high_scan), body, 0)

    def finish(block, carry):
        for copy in copies(block):
            copy.wait()
        return carry

    lax.fori_loop(0, s.blocks, finish, 0)


VM = pl.BlockSpec(memory_space=pltpu.VMEM)
HBM = pl.BlockSpec(memory_space=pltpu.HBM)
LIMIT = 6 * 1024 * 1024


def in_hbm(x):
    return pltpu.with_memory_space_constraint(x, pltpu.HBM)


def call(body, name, outs, scratch, args, passes, n_hbm=0, out_specs=None, aliases=()):
    work = int(passes * 16 * 128 * 2048)
    return pl.pallas_call(
        body,
        name=name,
        out_shape=outs,
        in_specs=[HBM] * n_hbm + [VM] * (len(args) - n_hbm),
        out_specs=out_specs or [VM] * len(outs),
        scratch_shapes=scratch,
        input_output_aliases=dict(aliases),
        cost_estimate=pl.CostEstimate(
            flops=work, bytes_accessed=work, transcendentals=0
        ),
        compiler_params=pltpu.CompilerParams(vmem_limit_bytes=LIMIT),
    )(*args)


def per_device(devices, rhs, rate, delta, b_proj, c_proj, skip, curvature, damping):
    tokens, columns = rhs.shape
    entries = rate.shape[0]
    s = Sizes(tokens, columns, entries, devices, STREAMS)
    held = pltpu.VMEM
    dma = pltpu.SemaphoreType.DMA
    every = range(STREAMS)
    per_token = held((s.blocks, s.steps, SUB, LANE), F32)
    expanded = (s.steps, entries, SUB, LANE)
    edge = held((s.blocks, entries, SUB, LANE), F32)
    half_state = held((s.half, s.steps, entries, 2, SUB, LANE), F32)
    tile = (s.blocks, tokens, LANE)
    packet = held((s.half + 1, entries, LANE), F32)
    linked = held((s.half, entries, LANE), F32)
    sums = held((2, SUB, LANE), F32)
    both = pltpu.VMEM((2, s.half + 1, entries, LANE), F32)
    joined = pltpu.VMEM((s.blocks, entries, LANE), F32)

    def swap(send, distance):
        pairs = [(device, device ^ distance) for device in range(devices)]
        return lax.ppermute(send, "seq", pairs)

    def kernel(body, *more):
        return functools.partial(body, s, *more)

    offsets = [s.blocks * g for g in every]
    firsts = [
        call(
            kernel(first_kernel, offsets[g]),
            f"first_{g}",
            [
                half_state, half_state, held(expanded, F32),
                held((s.blocks, SUB, LANE), F32), edge, packet, packet,
                held(tile, F32), held(tile, F32), held((entries, columns), F32),
                held((1, columns), F32), held((1, columns), F32),
            ],
            [
                pltpu.VMEM(tile, F32), pltpu.VMEM(expanded, F32),
                pltpu.VMEM((2, entries, tokens), F32),
                pltpu.VMEM((2, tokens, entries), F32),
                dma((s.blocks,)), dma((s.blocks,)), dma((s.blocks,)), dma((5,)),
            ],
            [
                in_hbm(x)
                for x in (
                    rhs, delta, curvature, rate, skip[None], damping[None],
                    b_proj.T, c_proj.T,
                )
            ],
            2,
            n_hbm=8,
        )
        for g in every
    ]
    (
        low_scan, high_scan, cx, total, e, keep, give, rhs_v, curv, rates, skips, damps,
    ) = zip(*firsts)

    def around(keep, give, backward, letter, known):
        (keep,), (give,) = keep, give
        first = known is None
        made = []
        got = swap(give, 1)
        outs = [packet] + [held((2, s.half, entries, LANE), F32)] * first
        chip = call(
            kernel(join_kernel, backward, first),
            f"join_{letter}",
            outs,
            [],
            (keep, got, rates[0] if first else known[0]),
            0.02,
        )
        core = chip[1] if first else known[0]
        group, arrive, passing = chip[0], None, None
        for level, (stride, radix) in enumerate(s.levels):
            last = level == len(s.levels) - 1
            packets = [group] + [swap(group, stride * k) for k in range(1, radix)]
            args = packets + [arrive] * (level > 0)
            args += [rates[0] if first else known[1 + level]]
            args += [passing] * (first and level > 0)
            outs = [linked, linked, sums] if last else [packet, linked]
            if last:
                args += [keep, got, core]
            if first:
                outs = outs + [
                    held((2, 2 * radix - 1, s.half, entries, LANE), F32),
                    held((2, s.half, LANE), F32),
                ]
            results = call(
                kernel(level_kernel, level, backward, first),
                f"level_{level}_{letter}",
                outs,
                [],
                args,
                0.02,
            )
            if first:
                *results, weights, passing = results
                made.append(weights)
            group, arrive = results[:2]
        own, give_back, total = results
        return (own, swap(give_back, 1)), [total], known or [core, *made]

    def common(g, e, arrive):
        return (low_scan[g], high_scan[g], cx[g], total[g], e[g], *arrive)

    def consts(g):
        return (rates[g], skips[g], damps[g])

    arrive, _, known = around(keep, give, False, "a", None)
    e, keep, give, w, y0 = zip(
        *[
            call(
                kernel(forward_kernel, offsets[g], True),
                f"forward_a_{g}",
                [edge, packet, packet, per_token, per_token],
                [both, joined],
                (rhs_v[g], curv[g], *consts(g), *common(g, e, arrive)),
                2,
            )
            for g in every
        ]
    )
    arrive, sums_b, _ = around(keep, give, True, "b", known)
    e, keep, give, r = zip(
        *[
            call(
                kernel(backward_kernel, offsets[g]),
                f"backward_a_{g}",
                [edge, packet, packet, per_token],
                [both, joined],
                (rhs_v[g], *consts(g), *common(g, e, arrive), w[g], *sums_b),
                2,
            )
            for g in every
        ]
    )
    arrive, sums_c, _ = around(keep, give, False, "c", known)
    e, keep, give, w, d = zip(
        *[
            call(
                kernel(forward_kernel, offsets[g], False),
                f"forward_b_{g}",
                [edge, packet, packet, per_token, per_token],
                [both, joined],
                (
                    rhs_v[g], curv[g], *consts(g), *common(g, e, arrive),
                    r[g], y0[g], *sums_b, *sums_c,
                ),
                2,
            )
            for g in every
        ]
    )
    arrive, sums_d, _ = around(keep, give, True, "d", known)
    outs = ()
    for g in every:
        args = (
            rhs_v[g], *consts(g), *common(g, e, arrive), w[g], r[g], d[g],
            *sums_b, *sums_c, *sums_d,
        )
        outs = pl.pallas_call(
            kernel(last_kernel, offsets[g]),
            name=f"backward_b_{g}",
            out_shape=[jax.ShapeDtypeStruct((tokens, columns), F32)] * 2,
            in_specs=[VM] * len(args) + [HBM] * len(outs),
            out_specs=[HBM] * 2,
            scratch_shapes=[
                pltpu.VMEM(tile, F32), pltpu.VMEM(tile, F32),
                dma((s.blocks,)), dma((s.blocks,)), joined,
            ],
            input_output_aliases={len(args): 0, len(args) + 1: 1} if outs else {},
            compiler_params=pltpu.CompilerParams(vmem_limit_bytes=LIMIT),
        )(*args, *outs)
    return tuple(outs)


def solution(mesh):
    placed = (
        P("seq", None),
        P(),
        P("seq", None),
        P("seq", None),
        P("seq", None),
        P(),
        P("seq", None),
        P(),
    )
    return jax.shard_map(
        functools.partial(per_device, mesh.shape["seq"]),
        mesh=mesh,
        in_specs=placed,
        out_specs=(P("seq", None), P("seq", None)),
        check_vma=False,
    )
```
